128 devices in a mesh: half: 2 (over y_hi), row: 8 (over y_lo, z), col: 8 (over x, core).
Axes of the slice: x: 4, y: 4 (y_hi: 2, y_lo: 2; y = y_hi * 2 + y_lo), z: 4, core: 2. Of those that a mesh axis runs over, the one named last changes fastest.
Arguments:
- child_block: bfloat16 [2, 8, 8, 256, 8, 8, 256], P('half', None, 'row', None, None, 'col'), may hold values from -6 to 6
- child_row: bfloat16 [2, 256, 8, 8, 256], P('half', 'row', None, 'col'), may hold values from -6 to 6
- child_col: bfloat16 [2, 256, 8, 8, 256], P('half', 'col', None, 'row'), may hold values from -0.375 to 0.375
- child_pivot_inv: bfloat16 [2, 256, 256], P('half'), may hold values from -0.375 to 0.375
- child_map: int32 [2, 64], replicated, may hold values from 0 to 126, as said below
- parent_row: bfloat16 [256, 8, 16, 256], P('row', None, ('half', 'col')), may hold values from -6 to 6
- parent_col: bfloat16 [256, 16, 8, 256], P(('half', 'col'), None, 'row'), may hold values from -0.375 to 0.375
- parent_pivot_inv: bfloat16 [256, 256], replicated, may hold values from -0.375 to 0.375
- parent_diag: float32 [16, 8, 256], P(None, 'row'), may hold values from 1 to 3
Outputs:
- schur: bfloat16 [16, 8, 256, 8, 16, 256], P(None, 'row', None, None, ('half', 'col'))
The draws below stay inside these ranges and needn't reach their ends.
Inputs may be any that keep to these rules, and one draw needn't show every extreme that they name: child_map[h, 8 * k + r] = 2 * 8 * k + r + p_h[k] for k and r from 0 to 7, where p_0 and p_1 are permutations of 0 to 7.
All inputs are finite; a program needn't handle non-finite values.
Results may differ from the reference program's by a relative error of at most 0.0041.
The reference program's roundings to bfloat16 on the way count: a program that leaves them out, or rounds other values in their place, can miss the bound.
Values may be sent and summed in bfloat16 or wider, within the bound.
A program may use at most 384 MiB of HBM per device.

```python
import jax
import jax.numpy as jnp
from jax import lax

TILE = 256
GRID = 8
CB_TILES = 64
PARENT_TILES = 128


def draw_child_map(key, part):
    mapped = []
    for sibling in range(2):
        shuffled = jax.random.permutation(jax.random.fold_in(key, 17 + sibling), GRID).astype(jnp.int32)
        blocks = jnp.arange(GRID, dtype=jnp.int32)
        offsets = 2 * GRID * blocks + shuffled
        mapped.append((offsets[:, None] + blocks[None, :]).reshape(-1))
    return jnp.stack(mapped).astype(jnp.int32)


def levels(stream_key, shape, split, low, high):
    def one(position, shards_of):
        heights = jax.random.uniform(jax.random.fold_in(jax.random.fold_in(stream_key, 6), position), (shards_of,), jnp.float32, low / len(split), high / len(split))
        return jnp.repeat(jnp.exp(heights), shape[position] // shards_of).reshape((-1,) + (1,) * (len(shape) - position - 1))

    gain = one(*split[0])
    for cut in split[1:]:
        gain = gain * one(*cut)
    return gain


def bell_draw(stream_key, extent, scale, reach, cuts=(), held_as=jnp.bfloat16):
    drawn = jax.random.normal(stream_key, extent, jnp.float32) * scale
    if len(cuts) > 0:
        drawn = levels(stream_key, extent, cuts, -0.22, 0.18) * drawn
    return jnp.clip(drawn, min=-reach, max=reach).astype(held_as)


def setup_inputs(seed: int = 0) -> dict:
    streams_of = jax.random.split(jax.random.key(seed), 10)
    return {
        "child_block": bell_draw(streams_of[0], (2, GRID, GRID, TILE, GRID, GRID, TILE), 1.0, 6.0, ((0, 2), (2, 8), (5, 8))),
        "child_row": bell_draw(streams_of[1], (2, TILE, GRID, GRID, TILE), 1.0, 6.0, ((0, 2), (1, 8), (3, 8))),
        "child_col": bell_draw(streams_of[2], (2, TILE, GRID, GRID, TILE), TILE ** -0.5, 0.375, ((0, 2), (1, 8), (3, 8))),
        "child_pivot_inv": bell_draw(streams_of[3], (2, TILE, TILE), TILE ** -0.5, 0.375, ((0, 2),)),
        "child_map": draw_child_map(jax.random.fold_in(streams_of[9], 71), 0),
        "parent_row": bell_draw(streams_of[5], (TILE, GRID, 2 * GRID, TILE), 1.0, 6.0, ((0, 8), (2, 16))),
        "parent_col": bell_draw(streams_of[6], (TILE, 2 * GRID, GRID, TILE), TILE ** -0.5, 0.375, ((0, 16), (2, 8))),
        "parent_pivot_inv": bell_draw(streams_of[7], (TILE, TILE), TILE ** -0.5, 0.375),
        "parent_diag": jnp.clip(1.0 + 2.0 * jax.random.uniform(streams_of[8], (2 * GRID, GRID, TILE), jnp.float32) ** levels(streams_of[8], (2 * GRID, GRID, TILE), ((1, 8),), -0.2, 0.2), 1.0, 3.0),
    }


def inverse_maps(child_map):
    targets = jnp.arange(PARENT_TILES, dtype=jnp.int32)
    matches = child_map[:, None, :] == targets[None, :, None]
    covered = jnp.any(matches, axis=2)
    positions = jnp.arange(CB_TILES, dtype=jnp.int32)
    sources = jnp.sum(jnp.where(matches, positions[None, None, :], 0), axis=2).astype(jnp.int32)
    return covered, sources


def reference(child_block, child_row, child_col, child_pivot_inv, child_map, parent_row, parent_col, parent_pivot_inv, parent_diag):
    contrib = TILE * CB_TILES
    order_total = TILE * PARENT_TILES
    blocks_all = child_block.reshape(2, contrib, contrib)
    cols_all = child_col.reshape(2, TILE, contrib)
    scaled_rows = jnp.stack([jnp.dot(child_pivot_inv[sibling], child_row[sibling].reshape(TILE, contrib), preferred_element_type=jnp.float32) for sibling in range(2)]).astype(jnp.bfloat16)
    parent_scaled = jnp.dot(parent_pivot_inv, parent_row.reshape(TILE, order_total), preferred_element_type=jnp.float32).astype(jnp.bfloat16)
    parent_cols = parent_col.reshape(TILE, order_total)
    diagonal = parent_diag.reshape(order_total)
    covered, sources = inverse_maps(child_map)
    identity = jnp.eye(TILE, dtype=jnp.float32)

    def tile_row(target):
        offset = target * TILE
        panel_cols = lax.dynamic_slice_in_dim(parent_cols, offset, TILE, 1)
        accumulated = -jnp.dot(panel_cols.T, parent_scaled, preferred_element_type=jnp.float32)
        diag_block = identity * lax.dynamic_slice_in_dim(diagonal, offset, TILE, 0)[:, None]
        current = lax.dynamic_slice_in_dim(accumulated, offset, TILE, 1)
        accumulated = lax.dynamic_update_slice_in_dim(accumulated, current + diag_block, offset, 1)
        for sibling in range(2):
            source = sources[sibling, target]
            first_row = source * TILE
            block_rows = lax.dynamic_slice_in_dim(blocks_all[sibling], first_row, TILE, 0)
            panel_child = lax.dynamic_slice_in_dim(cols_all[sibling], first_row, TILE, 1)
            update = jnp.dot(panel_child.T, scaled_rows[sibling], preferred_element_type=jnp.float32)
            contribution = (block_rows.astype(jnp.float32) - update).astype(jnp.bfloat16)
            contribution = lax.optimization_barrier(contribution)
            spread = jnp.zeros((TILE, PARENT_TILES, TILE), jnp.float32).at[:, child_map[sibling], :].set(contribution.reshape(TILE, CB_TILES, TILE).astype(jnp.float32))
            accumulated = accumulated + jnp.where(covered[sibling, target], spread.reshape(TILE, order_total), 0.0)
        return accumulated.astype(jnp.bfloat16)

    result = lax.map(tile_row, jnp.arange(PARENT_TILES, dtype=jnp.int32))
    return result.reshape(2 * GRID, GRID, TILE, GRID, 2 * GRID, TILE)
```

```python
import functools

import jax
import jax.numpy as jnp
from jax import lax
from jax.experimental import pallas as pl
from jax.experimental.pallas import tpu as pltpu
from jax.sharding import PartitionSpec as P

MESH = pl.DeviceIdType.MESH
T = 256
L = 128
G = 8
BF = jnp.bfloat16
F32 = jnp.float32

RELAYED = {
    (0, 0): (7,),
    (0, 1): (6, 7),
    (0, 3): (0, 1),
    (1, 1): (7,),
    (1, 2): (6, 7),
    (1, 3): (6, 7),
    (1, 7): (0, 1),
}
RELAYS = {}
for (_h, _c), _cols in RELAYED.items():
    for _v in _cols:
        RELAYS.setdefault((1 if _v < _c else 0, _c), []).append((_h, _v))
RELAY_SLOTS = max(len(v) for v in RELAYS.values())


def relay_route(h, c, target):
    relayed = h < 0
    slot = 0 * c
    for (hh, cc), cols in RELAYED.items():
        for v in cols:
            hit = (h == hh) & (c == cc) & (target == v)
            relayed = relayed | hit
            k = RELAYS[(1 if v < cc else 0, cc)].index((hh, v))
            if k:
                slot = jnp.where(hit, k, slot)
    return relayed, slot


def exchange_kernel(
    q_ref,
    block_hbm,
    crow_ref,
    ccol_ref,
    prow_ref,
    pcol_ref,
    cinv_ref,
    pinv_ref,
    recv_hbm,
    v_ref,
    pcol_hbm,
    stage,
    tile,
    plain,
    rowg,
    colg,
    colt,
    w,
    sbuf,
    lbuf,
    prowg,
    stage_sem,
    row_sem,
    col_sem,
    prow_sem,
    pcol_sem,
    ssem,
    rsem,
    lsem,
    fsem,
):
    h = lax.axis_index("half")
    r = lax.axis_index("row")
    c = lax.axis_index("col")
    slot_me = h * G + c

    def remote(src, dst, send, recv, dev):
        return pltpu.make_async_remote_copy(
            src_ref=src,
            dst_ref=dst,
            send_sem=send,
            recv_sem=recv,
            device_id=dev,
            device_id_type=MESH,
        )

    def fetch(k, s):
        return pltpu.make_async_copy(block_hbm.at[k], stage.at[s], stage_sem.at[s])

    fetch(0, 0).start()

    barrier = pltpu.get_barrier_semaphore()
    me = h * 64 + r * 8 + c

    def greet(i, _):
        @pl.when(i != me)
        def _():
            pl.semaphore_signal(
                barrier,
                inc=1,
                device_id=(i // 64, (i // 8) % 8, i % 8),
                device_id_type=MESH,
            )

        return 0

    lax.fori_loop(0, 128, greet, 0)
    pl.semaphore_wait(barrier, 127)

    row_part = pl.ds(pl.multiple_of(r * 32, 32), 32)
    col_part = pl.ds(pl.multiple_of(c * 32, 32), 32)
    pcol_part = pl.ds(pl.multiple_of(slot_me * 16, 16), 16)

    def send_child(t, _):
        remote(
            crow_ref, rowg.at[:, row_part, :], row_sem.at[0], row_sem.at[1], (h, (r + t) % G, c)
        ).start()
        remote(
            ccol_ref, colg.at[:, col_part, :], col_sem.at[0], col_sem.at[1], (h, r, (c + t) % G)
        ).start()
        return 0

    lax.fori_loop(1, G, send_child, 0)
    pltpu.make_async_copy(crow_ref, rowg.at[:, row_part, :], row_sem.at[1]).start()
    pltpu.make_async_copy(ccol_ref, colg.at[:, col_part, :], col_sem.at[1]).start()

    def send_prow(t, _):
        remote(
            prow_ref, prowg.at[:, row_part, :], prow_sem.at[0], prow_sem.at[1], (h, (r + t) % G, c)
        ).start()
        return 0

    lax.fori_loop(1, G, send_prow, 0)
    pltpu.make_async_copy(prow_ref, prowg.at[:, row_part, :], prow_sem.at[1]).start()

    def send_pcol(t, _):
        to = (slot_me + t) % (2 * G)
        remote(
            pcol_ref,
            pcol_hbm.at[:, pcol_part, :],
            pcol_sem.at[0],
            pcol_sem.at[1],
            (to // G, r, to % G),
        ).start()
        return 0

    lax.fori_loop(1, 2 * G, send_pcol, 0)
    pltpu.make_async_copy(pcol_ref, pcol_hbm.at[:, pcol_part, :], pcol_sem.at[1]).start()

    def split(k, _):
        s = k % 2

        @pl.when(k + 1 < G)
        def _():
            fetch(k + 1, 1 - s).start()

        fetch(k, s).wait()

        def widen(m, _):
            x = stage[s, pl.ds(pl.multiple_of(m * 32, 32), 32)]
            x = x.astype(F32).reshape(256, T)
            for lane in range(2):
                tile[lane, pl.ds(pl.multiple_of(m * 256, 256), 256), :] = x[:, lane * L : lane * L + L]
            return 0

        lax.fori_loop(0, 8, widen, 0)
        for kk in range(G):
            for lane in range(2):
                plain[k * G + kk, :, pl.ds(lane * L, L)] = tile[
                    lane, pl.ds(kk, T, stride=G), :
                ].astype(BF)
        return 0

    lax.fori_loop(0, G, split, 0)

    remote(rowg, rowg, row_sem.at[0], row_sem.at[1], (h, r, c)).wait_recv()

    def scale(k, _):
        w[k] = jnp.dot(cinv_ref[...], rowg[k], preferred_element_type=F32).astype(BF)
        return 0

    lax.fori_loop(0, G, scale, 0)
    remote(colg, colg, col_sem.at[0], col_sem.at[1], (h, r, c)).wait_recv()

    def turn(k, _):
        colt[k] = colg[k].T
        return 0

    lax.fori_loop(0, G, turn, 0)

    def block(i, _):
        d = (i // G + c) % G
        dd = (i + r) % G
        s = d * G + dd
        update = jnp.dot(colt[d], w[dd], preferred_element_type=F32)
        sbuf[s] = (plain[q_ref[d] * G + q_ref[dd]].astype(F32) - update).astype(BF)
        to = c + dd
        th, tr, tc = to // G, (r + d) % G, to % G
        relayed, slot = relay_route(h, c, tc)
        relayed = relayed & ((th != h) | (tr != r))
        here = (d == 0) & (to == slot_me)
        sent = jnp.where(s == 0, G, d)

        @pl.when(relayed)
        def _():
            remote(
                sbuf.at[s],
                lbuf.at[slot * G + r],
                ssem.at[sent],
                lsem.at[slot * G + r],
                (th, tr, c),
            ).start()

        @pl.when(jnp.logical_not(relayed | here))
        def _():
            remote(
                sbuf.at[s], recv_hbm.at[h, r, c], ssem.at[sent], rsem.at[h * G + c], (th, tr, tc)
            ).start()

        @pl.when(here)
        def _():
            pltpu.make_async_copy(sbuf.at[s], recv_hbm.at[h, r, c], rsem.at[h * G + c]).start()

        return 0

    lax.fori_loop(0, G * G, block, 0)

    for (rh, rc), passing in RELAYS.items():

        @pl.when((h == rh) & (c == rc))
        def _(rh=rh, passing=passing):
            def forward(i, _):
                d = (i + c) % G
                frm = (r - d + G) % G
                for slot, (hs, tc) in enumerate(passing):

                    def pass_on(slot=slot, hs=hs, tc=tc):
                        buf = lbuf.at[slot * G + frm]
                        remote(
                            buf, buf, fsem.at[slot], lsem.at[slot * G + frm], (1 - h, r, c)
                        ).wait_recv()
                        remote(
                            buf,
                            recv_hbm.at[hs, frm, c],
                            fsem.at[slot],
                            rsem.at[hs * G + c],
                            (h, r, tc),
                        ).start()

                    if hs == rh:
                        pl.when(d != 0)(pass_on)
                    else:
                        pass_on()
                return 0

            lax.fori_loop(0, G, forward, 0)

    remote(prowg, prowg, prow_sem.at[0], prow_sem.at[1], (h, r, c)).wait_recv()

    def pscale(k, _):
        v_ref[k] = jnp.dot(pinv_ref[...], prowg[k], preferred_element_type=F32).astype(BF)
        return 0

    lax.fori_loop(0, G, pscale, 0)

    seven = pl.ds(0, 7)
    other = (1 - h, r, c)
    remote(rowg.at[seven], rowg.at[seven], row_sem.at[0], row_sem.at[1], other).wait_send()
    remote(colg.at[seven], colg.at[seven], col_sem.at[0], col_sem.at[1], other).wait_send()
    remote(prowg.at[seven], prowg.at[seven], prow_sem.at[0], prow_sem.at[1], other).wait_send()
    fifteen = pl.ds(0, 15)
    remote(
        pcol_hbm.at[fifteen], pcol_hbm.at[fifteen], pcol_sem.at[0], pcol_sem.at[1], other
    ).wait_send()
    remote(pcol_hbm, pcol_hbm, pcol_sem.at[0], pcol_sem.at[1], other).wait_recv()

    for (rh, rc), passing in RELAYS.items():

        @pl.when((h == rh) & (c == rc))
        def _(rh=rh, passing=passing):
            for slot, (hs, _tc) in enumerate(passing):
                part = lbuf.at[pl.ds(0, G - 1 if hs == rh else G)]
                remote(part, part, fsem.at[slot], lsem.at[0], other).wait_send()

    part = sbuf.at[pl.ds(0, G - 1)]
    remote(part, part, ssem.at[0], rsem.at[0], other).wait_send()

    @pl.when(h == 1)
    def _():
        one = sbuf.at[pl.ds(0, 1)]
        remote(one, one, ssem.at[G], rsem.at[0], other).wait_send()

    for d in range(1, G):
        part = sbuf.at[pl.ds(0, G)]
        remote(part, part, ssem.at[d], rsem.at[0], other).wait_send()

    for hs in range(2):
        for cs in range(G):

            @pl.when((slot_me - cs >= 0) & (slot_me - cs < G))
            def _(hs=hs, cs=cs):
                dst = recv_hbm.at[hs, :, cs]
                remote(sbuf.at[pl.ds(0, G)], dst, ssem.at[0], rsem.at[hs * G + cs], other).wait_recv()


def exchange(q, block, crow, ccol, prow, pcol, cinv, pinv):
    any_space = pl.BlockSpec(memory_space=pl.ANY)
    vmem = pl.BlockSpec(memory_space=pltpu.VMEM)
    smem = pl.BlockSpec(memory_space=pltpu.SMEM)
    dma = pltpu.SemaphoreType.DMA
    return pl.pallas_call(
        exchange_kernel,
        out_shape=(
            jax.ShapeDtypeStruct((2, G, G, T, T), BF),
            jax.ShapeDtypeStruct((G, T, T), BF),
            jax.ShapeDtypeStruct((2 * G, T, T), BF),
        ),
        in_specs=[smem, any_space] + [vmem] * 6,
        out_specs=(any_space, vmem, any_space),
        scratch_shapes=[
            pltpu.VMEM((2, T, G, T), BF),
            pltpu.VMEM((2, T * G, L), F32),
            pltpu.VMEM((G * G, T, T), BF),
            pltpu.VMEM((G, T, T), BF),
            pltpu.VMEM((G, T, T), BF),
            pltpu.VMEM((G, T, T), BF),
            pltpu.VMEM((G, T, T), BF),
            pltpu.VMEM((G * G, T, T), BF),
            pltpu.VMEM((RELAY_SLOTS * G, T, T), BF),
            pltpu.VMEM((G, T, T), BF),
            dma((2,)),
            dma((2,)),
            dma((2,)),
            dma((2,)),
            dma((2,)),
            dma((G + 1,)),
            dma((2 * G,)),
            dma((RELAY_SLOTS * G,)),
            dma((RELAY_SLOTS,)),
        ],
        compiler_params=pltpu.CompilerParams(
            collective_id=0, has_side_effects=True, vmem_limit_bytes=48 << 20
        ),
        name="exchange",
    )(q, block, crow, ccol, prow, pcol, cinv, pinv)


def assemble_kernel(
    rows_ref, cols_ref, info_ref, from0, from1, v_ref, pcol_ref, diag_ref, out_ref, tile
):
    k = pl.program_id(0)
    odd = pl.program_id(1)
    pc = pcol_ref[0]
    for b in range(G):
        acc = -lax.dot_general(
            pc, v_ref[b], (((0,), (0,)), ((), ())), preferred_element_type=F32
        )
        for hs, part in ((0, from0), (1, from1)):
            cs = cols_ref[hs * G + b]
            live = (info_ref[2 * G + hs * G + k] == odd) & (cs >= 0) & (cs < G)
            piece = part[0, 0, jnp.clip(cs, 0, G - 1)].astype(F32)
            acc = acc + jnp.where(live, piece, 0.0)
        for lane in range(2):
            tile[lane, pl.ds(b, T, stride=G), :] = acc[:, lane * L : lane * L + L]

    @pl.when((info_ref[0] == 1) & (info_ref[1] == odd))
    def _():
        i = lax.broadcasted_iota(jnp.int32, (T, T), 0)
        j = lax.broadcasted_iota(jnp.int32, (T, T), 1)
        extra = jnp.where(i == j, diag_ref[0], 0.0)
        for b in range(G):

            @pl.when(k == b)
            def _():
                for lane in range(2):
                    tile[lane, pl.ds(b, T, stride=G), :] += extra[:, lane * L : lane * L + L]

    for m in range(8):
        for lane in range(2):
            out_ref[0, pl.ds(m * 32, 32), :, pl.ds(lane * L, L)] = (
                tile[lane, pl.ds(m * 256, 256), :].reshape(32, G, L).astype(BF)
            )


def assemble(rows, cols, info, recv, v, pcol, diag):
    whole = pl.BlockSpec((G, T, T), lambda k, o, *_: (0, 0, 0))
    return pl.pallas_call(
        assemble_kernel,
        out_shape=jax.ShapeDtypeStruct((2 * G, T, G, T), BF),
        grid_spec=pltpu.PrefetchScalarGridSpec(
            num_scalar_prefetch=3,
            grid=(G, 2),
            in_specs=[
                pl.BlockSpec((1, 1, G, T, T), lambda k, o, rows, *_: (0, rows[k], 0, 0, 0)),
                pl.BlockSpec((1, 1, G, T, T), lambda k, o, rows, *_: (1, rows[G + k], 0, 0, 0)),
                whole,
                pl.BlockSpec((1, T, T), lambda k, o, *_: (2 * k + o, 0, 0)),
                pl.BlockSpec((1, 1, T), lambda k, o, *_: (2 * k + o, 0, 0)),
            ],
            out_specs=pl.BlockSpec((1, T, G, T), lambda k, o, *_: (2 * k + o, 0, 0, 0)),
            scratch_shapes=[pltpu.VMEM((2, T * G, L), F32)],
        ),
        compiler_params=pltpu.CompilerParams(vmem_limit_bytes=48 << 20),
        name="assemble",
    )(rows, cols, info, recv, recv, v, pcol, diag)


def shards(
    child_block,
    child_row,
    child_col,
    child_pivot_inv,
    child_map,
    parent_row,
    parent_col,
    parent_pivot_inv,
    parent_diag,
):
    h = lax.axis_index("half")
    r = lax.axis_index("row")
    c = lax.axis_index("col")
    steps = jnp.arange(G, dtype=jnp.int32)
    shift = child_map.reshape(2, G, G)[:, :, 0] - 2 * G * steps[None, :]
    source = jnp.sum(
        jnp.where(shift[:, None, :] == steps[None, :, None], steps[None, None, :], 0), axis=2
    ).astype(jnp.int32)
    q = lax.dynamic_index_in_dim(source, h, 0, keepdims=False)

    def ordered(x):
        x = x.reshape(x.shape[1], G, T)
        return jnp.swapaxes(jnp.take(x, q, axis=1), 0, 1)

    crow = ordered(child_row)
    ccol = ordered(child_col)
    prow = jnp.swapaxes(parent_row.reshape(-1, G, T), 0, 1)
    pcol = jnp.swapaxes(parent_col.reshape(-1, 2 * G, T), 0, 1)
    recv, v, pcols = exchange(
        q,
        child_block.reshape(G, T, G, T),
        crow,
        ccol,
        prow,
        pcol,
        child_pivot_inv[0],
        parent_pivot_inv,
    )
    rows = ((r - shift) % G).reshape(-1)
    cols = (h * G + c - shift).reshape(-1)
    carry = (shift > r).astype(jnp.int32).reshape(-1)
    head = jnp.stack([(r == c).astype(jnp.int32), h.astype(jnp.int32)])
    info = jnp.concatenate([head, jnp.zeros((2 * G - 2,), jnp.int32), carry])
    out = assemble(rows, cols, info, recv, v, pcols, parent_diag)
    return out.reshape(2 * G, 1, T, G, 1, T)


def solution(mesh):
    return jax.shard_map(
        shards,
        mesh=mesh,
        in_specs=(
            P("half", None, "row", None, None, "col", None),
            P("half", "row", None, "col", None),
            P("half", "col", None, "row", None),
            P("half", None, None),
            P(),
            P("row", None, ("half", "col"), None),
            P(("half", "col"), None, "row", None),
            P(),
            P(None, "row", None),
        ),
        out_specs=P(None, "row", None, None, ("half", "col"), None),
        check_vma=False,
    )
```

```python
import functools

import jax
import jax.numpy as jnp
from jax import lax
from jax.experimental import pallas as pl
from jax.experimental.pallas import tpu as pltpu
from jax.sharding import PartitionSpec as P

MESH = pl.DeviceIdType.MESH
T = 256
L = 128
G = 8
BF = jnp.bfloat16
F32 = jnp.float32

RELAYED = {
    (0, 0): (7,),
    (0, 1): (6, 7),
    (0, 3): (0, 1),
    (1, 1): (7,),
    (1, 2): (6, 7),
    (1, 3): (6, 7),
    (1, 7): (0, 1),
}
RELAYS = {}
for (_h, _c), _cols in RELAYED.items():
    for _v in _cols:
        RELAYS.setdefault((1 if _v < _c else 0, _c), []).append((_h, _v))
RELAY_SLOTS = max(len(v) for v in RELAYS.values())


def relay_route(h, c, target):
    relayed = h < 0
    slot = 0 * c
    for (hh, cc), cols in RELAYED.items():
        for v in cols:
            hit = (h == hh) & (c == cc) & (target == v)
            relayed = relayed | hit
            k = RELAYS[(1 if v < cc else 0, cc)].index((hh, v))
            if k:
                slot = jnp.where(hit, k, slot)
    return relayed, slot


def turn_of(i):
    return i % G, (2 * (i // G) + i // (4 * G) + i) % G


def exchange_kernel(
    q_ref,
    block_hbm,
    crow_ref,
    ccol_ref,
    prow_ref,
    pcol_ref,
    cinv_ref,
    pinv_ref,
    recv_hbm,
    v_ref,
    pcol_hbm,
    stage,
    tile,
    plain,
    rowg,
    colg,
    colt,
    w,
    sbuf,
    lbuf,
    prowg,
    zeros,
    stage_sem,
    row_sem,
    col_sem,
    prow_sem,
    pcol_sem,
    ssem,
    rsem,
    lsem,
    fsem,
):
    h = lax.axis_index("half")
    r = lax.axis_index("row")
    c = lax.axis_index("col")
    slot_me = h * G + c

    def remote(src, dst, send, recv, dev):
        return pltpu.make_async_remote_copy(
            src_ref=src,
            dst_ref=dst,
            send_sem=send,
            recv_sem=recv,
            device_id=dev,
            device_id_type=MESH,
        )

    def fetch(k, s):
        return pltpu.make_async_copy(block_hbm.at[k], stage.at[s], stage_sem.at[s])

    fetch(0, 0).start()

    barrier = pltpu.get_barrier_semaphore()
    me = h * 64 + r * 8 + c

    def greet(i, _):
        @pl.when(i != me)
        def _():
            pl.semaphore_signal(
                barrier,
                inc=1,
                device_id=(i // 64, (i // 8) % 8, i % 8),
                device_id_type=MESH,
            )

        return 0

    lax.fori_loop(0, 128, greet, 0)
    pl.semaphore_wait(barrier, 127)

    other = (1 - h, r, c)
    pair = (h, (r + G // 2) % G, c)
    twin = (h, r, c + 1 - 2 * (c % 2))
    row_part = pl.ds(pl.multiple_of(r * 32, 32), 32)
    pair_part = pl.ds(pl.multiple_of((r + G // 2) % G * 32, 32), 32)

    def rows_out(panel, whole, sems):
        remote(panel, whole.at[:, row_part, :], sems.at[0], sems.at[2], pair).start()
        for t in range(1, 4):
            to = (h, r // 4 * 4 + (r + t) % 4, c)
            remote(panel, whole.at[:, row_part, :], sems.at[0], sems.at[3], to).start()
        pltpu.make_async_copy(panel, whole.at[:, row_part, :], sems.at[3]).start()

    def rows_on(whole, sems):
        part = whole.at[:, pair_part, :]
        remote(part, part, sems.at[0], sems.at[2], pair).wait_recv()
        for t in range(1, 4):
            to = (h, r // 4 * 4 + (r + t) % 4, c)
            remote(part, part, sems.at[1], sems.at[4], to).start()

    def rows_in(whole, sems):
        four, three = whole.at[pl.ds(0, 4)], whole.at[pl.ds(0, 3)]
        remote(four, four, sems.at[0], sems.at[3], pair).wait_recv()
        remote(three, three, sems.at[0], sems.at[4], pair).wait_recv()

    def rows_left(whole, sems):
        four, three = whole.at[pl.ds(0, 4)], whole.at[pl.ds(0, 3)]
        remote(four, four, sems.at[0], sems.at[3], pair).wait_send()
        remote(three, three, sems.at[1], sems.at[4], pair).wait_send()

    ccol_part = pl.ds(pl.multiple_of(c % 2 * 128 + c // 2 * 32, 32), 32)
    ccol_core = pl.ds(pl.multiple_of(c % 2 * 128, 128), 128)
    pcol_part = pl.ds(pl.multiple_of(c % 2 * 128 + h * 64 + c // 2 * 16, 16), 16)
    pcol_over = pl.ds(pl.multiple_of(c % 2 * 128 + (1 - h) * 64 + c // 2 * 16, 16), 16)
    pcol_core = pl.ds(pl.multiple_of(c % 2 * 128, 128), 128)

    rows_out(crow_ref, rowg, row_sem)
    for t in range(1, 4):
        to = (h, r, (c + 2 * t) % G)
        remote(ccol_ref, colg.at[:, ccol_part, :], col_sem.at[0], col_sem.at[2], to).start()
    pltpu.make_async_copy(ccol_ref, colg.at[:, ccol_part, :], col_sem.at[2]).start()
    remote(pcol_ref, pcol_hbm.at[:, pcol_part, :], pcol_sem.at[0], pcol_sem.at[3], other).start()
    rows_out(prow_ref, prowg, prow_sem)
    for t in range(1, 4):
        to = (h, r, (c + 2 * t) % G)
        remote(pcol_ref, pcol_hbm.at[:, pcol_part, :], pcol_sem.at[0], pcol_sem.at[4], to).start()
    pltpu.make_async_copy(pcol_ref, pcol_hbm.at[:, pcol_part, :], pcol_sem.at[4]).start()
    rows_on(rowg, row_sem)

    def split(k, _):
        s = k % 2

        @pl.when(k + 1 < G)
        def _():
            fetch(k + 1, 1 - s).start()

        fetch(k, s).wait()

        def widen(m, _):
            x = stage[s, pl.ds(pl.multiple_of(m * 32, 32), 32)]
            x = x.astype(F32).reshape(256, T)
            for lane in range(2):
                tile[lane, pl.ds(pl.multiple_of(m * 256, 256), 256), :] = x[:, lane * L : lane * L + L]
            return 0

        lax.fori_loop(0, 8, widen, 0)
        for kk in range(G):
            for lane in range(2):
                plain[k * G + kk, :, pl.ds(lane * L, L)] = tile[
                    lane, pl.ds(kk, T, stride=G), :
                ].astype(BF)
        return 0

    lax.fori_loop(0, G, split, 0)

    zeros[...] = jnp.zeros_like(zeros)
    half_part = colg.at[:, ccol_core, :]
    remote(half_part, half_part, col_sem.at[0], col_sem.at[2], twin).wait_recv()
    remote(half_part, half_part, col_sem.at[1], col_sem.at[3], twin).start()
    rows_on(prowg, prow_sem)
    part = pcol_hbm.at[:, pcol_over, :]
    remote(part, part, pcol_sem.at[0], pcol_sem.at[3], other).wait_recv()
    for t in range(1, 4):
        to = (h, r, (c + 2 * t) % G)
        remote(part, part, pcol_sem.at[1], pcol_sem.at[5], to).start()

    rows_in(rowg, row_sem)

    def scale(k, _):
        w[k] = jnp.dot(cinv_ref[...], rowg[k], preferred_element_type=F32).astype(BF)
        return 0

    lax.fori_loop(0, G, scale, 0)
    remote(half_part, half_part, col_sem.at[1], col_sem.at[3], twin).wait_recv()

    def turn(k, _):
        colt[k] = colg[k].T
        return 0

    lax.fori_loop(0, G, turn, 0)

    def block(i, _):
        d, dd = turn_of(i)
        s = d * G + dd
        update = jnp.dot(colt[d], w[dd], preferred_element_type=F32)
        sbuf[s] = (plain[q_ref[d] * G + q_ref[dd]].astype(F32) - update).astype(BF)
        to = c + dd
        th, tr, tc = to // G, (r + d) % G, to % G
        relayed, slot = relay_route(h, c, tc)
        relayed = relayed & ((th != h) | (tr != r))
        here = (d == 0) & (to == slot_me)
        sent = jnp.where(s == 0, G, d)

        @pl.when(relayed)
        def _():
            remote(
                sbuf.at[s],
                lbuf.at[slot * G + r],
                ssem.at[sent],
                lsem.at[slot * G + r],
                (th, tr, c),
            ).start()

        @pl.when(jnp.logical_not(relayed | here))
        def _():
            remote(
                sbuf.at[s], recv_hbm.at[h, r, c], ssem.at[sent], rsem.at[h * G + c], (th, tr, tc)
            ).start()

        @pl.when(here)
        def _():
            pltpu.make_async_copy(sbuf.at[s], recv_hbm.at[h, r, c], rsem.at[h * G + c]).start()

        return 0

    lax.fori_loop(0, G * G, block, 0)

    four = pcol_hbm.at[pl.ds(0, 4)]
    three = pcol_hbm.at[pl.ds(0, 3)]
    remote(four, four, pcol_sem.at[0], pcol_sem.at[4], other).wait_recv()
    remote(three, three, pcol_sem.at[0], pcol_sem.at[5], other).wait_recv()
    part = pcol_hbm.at[:, pcol_core, :]
    remote(part, part, pcol_sem.at[2], pcol_sem.at[6], twin).start()

    for hs in range(2):
        for cs in range(G):

            @pl.when((slot_me - cs < 0) | (slot_me - cs >= G))
            def _(hs=hs, cs=cs):
                pltpu.make_async_copy(zeros, recv_hbm.at[hs, :, cs], rsem.at[hs * G + cs]).start()

    for (rh, rc), passing in RELAYS.items():

        @pl.when((h == rh) & (c == rc))
        def _(rh=rh, rc=rc, passing=passing):
            def forward(i, _):
                d, dd = turn_of(i)
                frm = (r - d + G) % G
                for slot, (hs, tc) in enumerate(passing):
                    due = dd == (tc - rc) % G
                    if hs == rh:
                        due = due & (d != 0)

                    @pl.when(due)
                    def _(slot=slot, hs=hs, tc=tc):
                        buf = lbuf.at[slot * G + frm]
                        remote(
                            buf, buf, fsem.at[slot], lsem.at[slot * G + frm], (1 - h, r, c)
                        ).wait_recv()
                        remote(
                            buf,
                            recv_hbm.at[hs, frm, c],
                            fsem.at[slot],
                            rsem.at[hs * G + c],
                            (h, r, tc),
                        ).start()

                return 0

            lax.fori_loop(0, G * G, forward, 0)

    rows_in(prowg, prow_sem)

    def pscale(k, _):
        v_ref[k] = -jnp.dot(pinv_ref[...], prowg[k], preferred_element_type=F32).astype(BF)
        return 0

    lax.fori_loop(0, G, pscale, 0)

    rows_left(rowg, row_sem)
    rows_left(prowg, prow_sem)
    quarter = colg.at[:, pl.ds(0, 96), :]
    remote(quarter, quarter, col_sem.at[0], col_sem.at[2], twin).wait_send()
    remote(half_part, half_part, col_sem.at[1], col_sem.at[3], twin).wait_send()
    remote(four, four, pcol_sem.at[0], pcol_sem.at[3], twin).wait_send()
    remote(three, three, pcol_sem.at[1], pcol_sem.at[3], twin).wait_send()
    part = pcol_hbm.at[:, pcol_core, :]
    remote(part, part, pcol_sem.at[2], pcol_sem.at[6], twin).wait_send()
    remote(part, part, pcol_sem.at[2], pcol_sem.at[6], twin).wait_recv()

    for (rh, rc), passing in RELAYS.items():

        @pl.when((h == rh) & (c == rc))
        def _(rh=rh, passing=passing):
            for slot, (hs, _tc) in enumerate(passing):
                part = lbuf.at[pl.ds(0, G - 1 if hs == rh else G)]
                remote(part, part, fsem.at[slot], lsem.at[0], other).wait_send()

    part = sbuf.at[pl.ds(0, G - 1)]
    remote(part, part, ssem.at[0], rsem.at[0], other).wait_send()

    @pl.when(h == 1)
    def _():
        one = sbuf.at[pl.ds(0, 1)]
        remote(one, one, ssem.at[G], rsem.at[0], other).wait_send()

    for d in range(1, G):
        part = sbuf.at[pl.ds(0, G)]
        remote(part, part, ssem.at[d], rsem.at[0], other).wait_send()

    for hs in range(2):
        for cs in range(G):
            dst = recv_hbm.at[hs, :, cs]
            remote(sbuf.at[pl.ds(0, G)], dst, ssem.at[0], rsem.at[hs * G + cs], other).wait_recv()


def exchange(q, block, crow, ccol, prow, pcol, cinv, pinv):
    any_space = pl.BlockSpec(memory_space=pl.ANY)
    vmem = pl.BlockSpec(memory_space=pltpu.VMEM)
    smem = pl.BlockSpec(memory_space=pltpu.SMEM)
    dma = pltpu.SemaphoreType.DMA
    return pl.pallas_call(
        exchange_kernel,
        out_shape=(
            pltpu.VMEM((2, G, G, T, T), BF),
            pltpu.VMEM((G, T, T), BF),
            pltpu.VMEM((2 * G, T, T), BF),
        ),
        in_specs=[smem, any_space] + [vmem] * 6,
        out_specs=(any_space, vmem, any_space),
        scratch_shapes=[
            pltpu.VMEM((2, T, G, T), BF),
            pltpu.VMEM((2, T * G, L), F32),
            pltpu.VMEM((G * G, T, T), BF),
            pltpu.VMEM((G, T, T), BF),
            pltpu.VMEM((G, T, T), BF),
            pltpu.VMEM((G, T, T), BF),
            pltpu.VMEM((G, T, T), BF),
            pltpu.VMEM((G * G, T, T), BF),
            pltpu.VMEM((RELAY_SLOTS * G, T, T), BF),
            pltpu.VMEM((G, T, T), BF),
            pltpu.VMEM((G, T, T), BF),
            dma((2,)),
            dma((5,)),
            dma((4,)),
            dma((5,)),
            dma((7,)),
            dma((G + 1,)),
            dma((2 * G,)),
            dma((RELAY_SLOTS * G,)),
            dma((RELAY_SLOTS,)),
        ],
        compiler_params=pltpu.CompilerParams(
            collective_id=0, has_side_effects=True, vmem_limit_bytes=34 << 20
        ),
        name="exchange",
    )(q, block, crow, ccol, prow, pcol, cinv, pinv)


def assemble_kernel(
    rows_ref, cols_ref, info_ref, recv_ref, v_ref, pcol_ref, diag_ref, out_ref, tile
):
    k = pl.program_id(0)
    odd = pl.program_id(1)
    live = [info_ref[2 + hs * G + k] == odd for hs in range(2)]

    def fill(parts):
        pc = pcol_ref[0].T
        for b in range(G):
            acc = jnp.dot(pc, v_ref[b], preferred_element_type=F32)
            for hs in parts:
                acc = acc + recv_ref[hs, rows_ref[hs * G + k], cols_ref[hs * G + b]].astype(F32)
            for lane in range(2):
                tile[lane, pl.ds(b, T, stride=G), :] = acc[:, lane * L : lane * L + L]

    pl.when(live[0] & live[1])(lambda: fill((0, 1)))
    pl.when(live[0] & jnp.logical_not(live[1]))(lambda: fill((0,)))
    pl.when(live[1] & jnp.logical_not(live[0]))(lambda: fill((1,)))
    pl.when(jnp.logical_not(live[0] | live[1]))(lambda: fill(()))

    @pl.when((info_ref[0] == 1) & (info_ref[1] == odd))
    def _():
        i = lax.broadcasted_iota(jnp.int32, (T, T), 0)
        j = lax.broadcasted_iota(jnp.int32, (T, T), 1)
        extra = jnp.where(i == j, diag_ref[0], 0.0)
        for lane in range(2):
            tile[lane, pl.ds(k, T, stride=G), :] += extra[:, lane * L : lane * L + L]

    for m in range(8):
        for lane in range(2):
            out_ref[0, pl.ds(m * 32, 32), :, pl.ds(lane * L, L)] = (
                tile[lane, pl.ds(m * 256, 256), :].reshape(32, G, L).astype(BF)
            )


def assemble(rows, cols, info, recv, v, pcol, diag):
    whole = pl.BlockSpec((G, T, T), lambda k, o, *_: (0, 0, 0))
    recv, v, pcol = (pltpu.with_memory_space_constraint(x, pltpu.VMEM) for x in (recv, v, pcol))
    return pl.pallas_call(
        assemble_kernel,
        out_shape=jax.ShapeDtypeStruct((2 * G, T, G, T), BF),
        grid_spec=pltpu.PrefetchScalarGridSpec(
            num_scalar_prefetch=3,
            grid=(G, 2),
            in_specs=[
                pl.BlockSpec(memory_space=pltpu.VMEM),
                whole,
                pl.BlockSpec((1, T, T), lambda k, o, *_: (2 * k + o, 0, 0)),
                pl.BlockSpec((1, 1, T), lambda k, o, *_: (2 * k + o, 0, 0)),
            ],
            out_specs=pl.BlockSpec((1, T, G, T), lambda k, o, *_: (2 * k + o, 0, 0, 0)),
            scratch_shapes=[pltpu.VMEM((2, T * G, L), F32)],
        ),
        compiler_params=pltpu.CompilerParams(vmem_limit_bytes=12 << 20),
        name="assemble",
    )(rows, cols, info, recv, v, pcol, diag)


def shards(
    child_block,
    child_row,
    child_col,
    child_pivot_inv,
    child_map,
    parent_row,
    parent_col,
    parent_pivot_inv,
    parent_diag,
):
    h = lax.axis_index("half")
    r = lax.axis_index("row")
    c = lax.axis_index("col")
    steps = jnp.arange(G, dtype=jnp.int32)
    shift = child_map.reshape(2, G, G)[:, :, 0] - 2 * G * steps[None, :]
    source = jnp.sum(
        jnp.where(shift[:, None, :] == steps[None, :, None], steps[None, None, :], 0), axis=2
    ).astype(jnp.int32)
    q = lax.dynamic_index_in_dim(source, h, 0, keepdims=False)

    def ordered(x):
        x = x.reshape(x.shape[1], G, T)
        return jnp.swapaxes(jnp.take(x, q, axis=1), 0, 1)

    crow = ordered(child_row)
    ccol = ordered(child_col)
    prow = jnp.swapaxes(parent_row.reshape(-1, G, T), 0, 1)
    pcol = jnp.swapaxes(parent_col.reshape(-1, 2 * G, T), 0, 1)
    cinv = jnp.swapaxes(child_pivot_inv.reshape(4, 2, 32, T), 0, 1).reshape(T, T)
    pinv = jnp.transpose(parent_pivot_inv.reshape(2, 4, 2, 16, T), (2, 0, 1, 3, 4)).reshape(T, T)
    recv, v, pcols = exchange(
        q, child_block.reshape(G, T, G, T), crow, ccol, prow, pcol, cinv, pinv
    )
    rows = ((r - shift) % G).reshape(-1)
    cols = ((c - shift) % G).reshape(-1)
    carry = (shift > r).astype(jnp.int32).reshape(-1)
    head = jnp.stack([(r == c).astype(jnp.int32), h.astype(jnp.int32)])
    info = jnp.concatenate([head, carry])
    out = assemble(rows, cols, info, recv, v, pcols, parent_diag)
    return out.reshape(2 * G, 1, T, G, 1, T)


def solution(mesh):
    return jax.shard_map(
        shards,
        mesh=mesh,
        in_specs=(
            P("half", None, "row", None, None, "col", None),
            P("half", "row", None, "col", None),
            P("half", "col", None, "row", None),
            P("half", None, None),
            P(),
            P("row", None, ("half", "col"), None),
            P(("half", "col"), None, "row", None),
            P(),
            P(None, "row", None),
        ),
        out_specs=P(None, "row", None, None, ("half", "col"), None),
        check_vma=False,
    )
```

```python
import functools

import jax
import jax.numpy as jnp
from jax import lax
from jax.experimental import pallas as pl
from jax.experimental.pallas import tpu as pltpu
from jax.sharding import PartitionSpec as P

MESH = pl.DeviceIdType.MESH
T = 256
L = 128
G = 8
BF = jnp.bfloat16
F32 = jnp.float32

RELAYED = {
    (0, 0): (2, 6, 7),
    (0, 1): (4, 6, 7),
    (0, 2): (0, 7),
    (0, 3): (1, 4, 7),
    (0, 5): (3,),
    (0, 6): (0, 3),
    (0, 7): (0,),
    (1, 0): (7,),
    (1, 1): (5, 7),
    (1, 2): (6,),
    (1, 3): (5,),
    (1, 4): (0, 1, 6),
    (1, 6): (1, 3),
    (1, 7): (0, 1, 2),
}
RELAYS = {}
for (_h, _c), _cols in RELAYED.items():
    for _v in _cols:
        RELAYS.setdefault((1 if _v < _c else 0, _c), []).append((_h, _v))
RELAY_SLOTS = max(len(v) for v in RELAYS.values())


def relay_route(h, c, target):
    relayed = h < 0
    slot = 0 * c
    for (hh, cc), cols in RELAYED.items():
        for v in cols:
            hit = (h == hh) & (c == cc) & (target == v)
            relayed = relayed | hit
            k = RELAYS[(1 if v < cc else 0, cc)].index((hh, v))
            if k:
                slot = jnp.where(hit, k, slot)
    return relayed, slot


def turn_of(i):
    return 3 * i % G, (2 * (i // G) + i // (4 * G) + i) % G


def exchange_kernel(
    q_ref,
    block_hbm,
    crow_ref,
    ccol_ref,
    prow_ref,
    pcol_ref,
    cinv_ref,
    pinv_ref,
    recv_hbm,
    v_ref,
    pcol_hbm,
    stage,
    tile,
    plain,
    rowg,
    colg,
    colt,
    w,
    sbuf,
    lbuf,
    prowg,
    zeros,
    stage_sem,
    row_sem,
    col_sem,
    prow_sem,
    pcol_sem,
    ssem,
    rsem,
    lsem,
    fsem,
):
    h = lax.axis_index("half")
    r = lax.axis_index("row")
    c = lax.axis_index("col")
    slot_me = h * G + c

    def remote(src, dst, send, recv, dev):
        return pltpu.make_async_remote_copy(
            src_ref=src,
            dst_ref=dst,
            send_sem=send,
            recv_sem=recv,
            device_id=dev,
            device_id_type=MESH,
        )

    def fetch(k, s):
        return pltpu.make_async_copy(block_hbm.at[k], stage.at[s], stage_sem.at[s])

    fetch(0, 0).start()

    barrier = pltpu.get_barrier_semaphore()
    me = h * 64 + r * 8 + c

    def greet(i, _):
        @pl.when(i != me)
        def _():
            pl.semaphore_signal(
                barrier,
                inc=1,
                device_id=(i // 64, (i // 8) % 8, i % 8),
                device_id_type=MESH,
            )

        return 0

    lax.fori_loop(0, 128, greet, 0)
    pl.semaphore_wait(barrier, 127)

    other = (1 - h, r, c)
    pair = (h, (r + G // 2) % G, c)
    twin = (h, r, c + 1 - 2 * (c % 2))
    row_part = pl.ds(pl.multiple_of(r * 32, 32), 32)
    pair_part = pl.ds(pl.multiple_of((r + G // 2) % G * 32, 32), 32)

    def rows_out(panel, whole, sems):
        remote(panel, whole.at[:, row_part, :], sems.at[0], sems.at[2], pair).start()
        for t in range(1, 4):
            to = (h, r // 4 * 4 + (r + t) % 4, c)
            remote(panel, whole.at[:, row_part, :], sems.at[0], sems.at[3], to).start()
        pltpu.make_async_copy(panel, whole.at[:, row_part, :], sems.at[3]).start()

    def rows_on(whole, sems):
        part = whole.at[:, pair_part, :]
        remote(part, part, sems.at[0], sems.at[2], pair).wait_recv()
        for t in range(1, 4):
            to = (h, r // 4 * 4 + (r + t) % 4, c)
            remote(part, part, sems.at[1], sems.at[4], to).start()

    def rows_in(whole, sems):
        four, three = whole.at[pl.ds(0, 4)], whole.at[pl.ds(0, 3)]
        remote(four, four, sems.at[0], sems.at[3], pair).wait_recv()
        remote(three, three, sems.at[0], sems.at[4], pair).wait_recv()

    def rows_left(whole, sems):
        four, three = whole.at[pl.ds(0, 4)], whole.at[pl.ds(0, 3)]
        remote(four, four, sems.at[0], sems.at[3], pair).wait_send()
        remote(three, three, sems.at[1], sems.at[4], pair).wait_send()

    ccol_part = pl.ds(pl.multiple_of(c % 2 * 128 + c // 2 * 32, 32), 32)
    ccol_core = pl.ds(pl.multiple_of(c % 2 * 128, 128), 128)
    pcol_part = pl.ds(pl.multiple_of(c % 2 * 128 + h * 64 + c // 2 * 16, 16), 16)
    pcol_over = pl.ds(pl.multiple_of(c % 2 * 128 + (1 - h) * 64 + c // 2 * 16, 16), 16)
    pcol_core = pl.ds(pl.multiple_of(c % 2 * 128, 128), 128)

    rows_out(crow_ref, rowg, row_sem)
    for t in range(1, 4):
        to = (h, r, (c + 2 * t) % G)
        remote(ccol_ref, colg.at[:, ccol_part, :], col_sem.at[0], col_sem.at[2], to).start()
    pltpu.make_async_copy(ccol_ref, colg.at[:, ccol_part, :], col_sem.at[2]).start()
    remote(pcol_ref, pcol_hbm.at[:, pcol_part, :], pcol_sem.at[0], pcol_sem.at[3], other).start()
    rows_out(prow_ref, prowg, prow_sem)
    for t in range(1, 4):
        to = (h, r, (c + 2 * t) % G)
        remote(pcol_ref, pcol_hbm.at[:, pcol_part, :], pcol_sem.at[0], pcol_sem.at[4], to).start()
    pltpu.make_async_copy(pcol_ref, pcol_hbm.at[:, pcol_part, :], pcol_sem.at[4]).start()
    rows_on(rowg, row_sem)

    def split(k, _):
        s = k % 2

        @pl.when(k + 1 < G)
        def _():
            fetch(k + 1, 1 - s).start()

        fetch(k, s).wait()

        def widen(m, _):
            x = stage[s, pl.ds(pl.multiple_of(m * 32, 32), 32)]
            x = x.astype(F32).reshape(256, T)
            for lane in range(2):
                tile[lane, pl.ds(pl.multiple_of(m * 256, 256), 256), :] = x[:, lane * L : lane * L + L]
            return 0

        lax.fori_loop(0, 8, widen, 0)
        for kk in range(G):
            for lane in range(2):
                plain[k * G + kk, :, pl.ds(lane * L, L)] = tile[
                    lane, pl.ds(kk, T, stride=G), :
                ].astype(BF)
        return 0

    lax.fori_loop(0, G, split, 0)

    zeros[...] = jnp.zeros_like(zeros)
    half_part = colg.at[:, ccol_core, :]
    remote(half_part, half_part, col_sem.at[0], col_sem.at[2], twin).wait_recv()
    remote(half_part, half_part, col_sem.at[1], col_sem.at[3], twin).start()
    rows_on(prowg, prow_sem)
    part = pcol_hbm.at[:, pcol_over, :]
    remote(part, part, pcol_sem.at[0], pcol_sem.at[3], other).wait_recv()
    for t in range(1, 4):
        to = (h, r, (c + 2 * t) % G)
        remote(part, part, pcol_sem.at[1], pcol_sem.at[5], to).start()

    rows_in(rowg, row_sem)

    def scale(k, _):
        w[k] = jnp.dot(cinv_ref[...], rowg[k], preferred_element_type=F32).astype(BF)
        return 0

    lax.fori_loop(0, G, scale, 0)
    remote(half_part, half_part, col_sem.at[1], col_sem.at[3], twin).wait_recv()

    def turn(k, _):
        colt[k] = colg[k].T
        return 0

    lax.fori_loop(0, G, turn, 0)

    def block(i, _):
        d, dd = turn_of(i % (G * G))
        s = d * G + dd
        to = c + dd
        th, tr, tc = to // G, (r + d) % G, to % G
        relayed, slot = relay_route(h, c, tc)
        relayed = relayed & ((th != h) | (tr != r))
        here = (d == 0) & (to == slot_me)
        sent = jnp.where(s == 0, G, d)

        def make():
            update = jnp.dot(colt[d], w[dd], preferred_element_type=F32)
            sbuf[s] = (plain[q_ref[d] * G + q_ref[dd]].astype(F32) - update).astype(BF)

        @pl.when(relayed & (i < G * G))
        def _():
            make()
            remote(
                sbuf.at[s],
                lbuf.at[slot * G + r],
                ssem.at[sent],
                lsem.at[slot * G + r],
                (th, tr, c),
            ).start()

        @pl.when(jnp.logical_not(relayed) & (i >= G * G))
        def _():
            make()

            @pl.when(jnp.logical_not(here))
            def _():
                remote(
                    sbuf.at[s],
                    recv_hbm.at[h, r, c],
                    ssem.at[sent],
                    rsem.at[h * G + c],
                    (th, tr, tc),
                ).start()

            @pl.when(here)
            def _():
                pltpu.make_async_copy(sbuf.at[s], recv_hbm.at[h, r, c], rsem.at[h * G + c]).start()

        return 0

    lax.fori_loop(0, 2 * G * G, block, 0)

    four = pcol_hbm.at[pl.ds(0, 4)]
    three = pcol_hbm.at[pl.ds(0, 3)]
    remote(four, four, pcol_sem.at[0], pcol_sem.at[4], other).wait_recv()
    remote(three, three, pcol_sem.at[0], pcol_sem.at[5], other).wait_recv()
    part = pcol_hbm.at[:, pcol_core, :]
    remote(part, part, pcol_sem.at[2], pcol_sem.at[6], twin).start()

    for hs in range(2):
        for cs in range(G):

            @pl.when((slot_me - cs < 0) | (slot_me - cs >= G))
            def _(hs=hs, cs=cs):
                pltpu.make_async_copy(zeros, recv_hbm.at[hs, :, cs], rsem.at[hs * G + cs]).start()

    for (rh, rc), passing in RELAYS.items():

        @pl.when((h == rh) & (c == rc))
        def _(rh=rh, rc=rc, passing=passing):
            def forward(i, _):
                d, dd = turn_of(i)
                frm = (r - d + G) % G
                for slot, (hs, tc) in enumerate(passing):
                    due = dd == (tc - rc) % G
                    if hs == rh:
                        due = due & (d != 0)

                    @pl.when(due)
                    def _(slot=slot, hs=hs, tc=tc):
                        buf = lbuf.at[slot * G + frm]
                        remote(
                            buf, buf, fsem.at[slot], lsem.at[slot * G + frm], (1 - h, r, c)
                        ).wait_recv()
                        remote(
                            buf,
                            recv_hbm.at[hs, frm, c],
                            fsem.at[slot],
                            rsem.at[hs * G + c],
                            (h, r, tc),
                        ).start()

                return 0

            lax.fori_loop(0, G * G, forward, 0)

    rows_in(prowg, prow_sem)

    def pscale(k, _):
        v_ref[k] = -jnp.dot(pinv_ref[...], prowg[k], preferred_element_type=F32).astype(BF)
        return 0

    lax.fori_loop(0, G, pscale, 0)

    rows_left(rowg, row_sem)
    rows_left(prowg, prow_sem)
    quarter = colg.at[:, pl.ds(0, 96), :]
    remote(quarter, quarter, col_sem.at[0], col_sem.at[2], twin).wait_send()
    remote(half_part, half_part, col_sem.at[1], col_sem.at[3], twin).wait_send()
    remote(four, four, pcol_sem.at[0], pcol_sem.at[3], twin).wait_send()
    remote(three, three, pcol_sem.at[1], pcol_sem.at[3], twin).wait_send()
    part = pcol_hbm.at[:, pcol_core, :]
    remote(part, part, pcol_sem.at[2], pcol_sem.at[6], twin).wait_send()
    remote(part, part, pcol_sem.at[2], pcol_sem.at[6], twin).wait_recv()

    for (rh, rc), passing in RELAYS.items():

        @pl.when((h == rh) & (c == rc))
        def _(rh=rh, passing=passing):
            for slot, (hs, _tc) in enumerate(passing):
                part = lbuf.at[pl.ds(0, G - 1 if hs == rh else G)]
                remote(part, part, fsem.at[slot], lsem.at[0], other).wait_send()

    part = sbuf.at[pl.ds(0, G - 1)]
    remote(part, part, ssem.at[0], rsem.at[0], other).wait_send()

    @pl.when(h == 1)
    def _():
        one = sbuf.at[pl.ds(0, 1)]
        remote(one, one, ssem.at[G], rsem.at[0], other).wait_send()

    for d in range(1, G):
        part = sbuf.at[pl.ds(0, G)]
        remote(part, part, ssem.at[d], rsem.at[0], other).wait_send()

    for hs in range(2):
        for cs in range(G):
            dst = recv_hbm.at[hs, :, cs]
            remote(sbuf.at[pl.ds(0, G)], dst, ssem.at[0], rsem.at[hs * G + cs], other).wait_recv()


def exchange(q, block, crow, ccol, prow, pcol, cinv, pinv):
    any_space = pl.BlockSpec(memory_space=pl.ANY)
    vmem = pl.BlockSpec(memory_space=pltpu.VMEM)
    smem = pl.BlockSpec(memory_space=pltpu.SMEM)
    dma = pltpu.SemaphoreType.DMA
    return pl.pallas_call(
        exchange_kernel,
        out_shape=(
            pltpu.VMEM((2, G, G, T, T), BF),
            pltpu.VMEM((G, T, T), BF),
            pltpu.VMEM((2 * G, T, T), BF),
        ),
        in_specs=[smem, any_space] + [vmem] * 6,
        out_specs=(any_space, vmem, any_space),
        scratch_shapes=[
            pltpu.VMEM((2, T, G, T), BF),
            pltpu.VMEM((2, T * G, L), F32),
            pltpu.VMEM((G * G, T, T), BF),
            pltpu.VMEM((G, T, T), BF),
            pltpu.VMEM((G, T, T), BF),
            pltpu.VMEM((G, T, T), BF),
            pltpu.VMEM((G, T, T), BF),
            pltpu.VMEM((G * G, T, T), BF),
            pltpu.VMEM((RELAY_SLOTS * G, T, T), BF),
            pltpu.VMEM((G, T, T), BF),
            pltpu.VMEM((G, T, T), BF),
            dma((2,)),
            dma((5,)),
            dma((4,)),
            dma((5,)),
            dma((7,)),
            dma((G + 1,)),
            dma((2 * G,)),
            dma((RELAY_SLOTS * G,)),
            dma((RELAY_SLOTS,)),
        ],
        compiler_params=pltpu.CompilerParams(
            collective_id=0, has_side_effects=True, vmem_limit_bytes=36 << 20
        ),
        name="exchange",
    )(q, block, crow, ccol, prow, pcol, cinv, pinv)


def assemble_kernel(
    rows_ref, cols_ref, info_ref, recv_ref, v_ref, pcol_ref, diag_ref, out_ref, tile
):
    k = pl.program_id(0)
    odd = pl.program_id(1)
    live = [info_ref[2 + hs * G + k] == odd for hs in range(2)]

    def fill(parts):
        pc = pcol_ref[0].T
        for b in range(G):
            acc = jnp.dot(pc, v_ref[b], preferred_element_type=F32)
            for hs in parts:
                acc = acc + recv_ref[hs, rows_ref[hs * G + k], cols_ref[hs * G + b]].astype(F32)
            for lane in range(2):
                tile[lane, pl.ds(b, T, stride=G), :] = acc[:, lane * L : lane * L + L]

    pl.when(live[0] & live[1])(lambda: fill((0, 1)))
    pl.when(live[0] & jnp.logical_not(live[1]))(lambda: fill((0,)))
    pl.when(live[1] & jnp.logical_not(live[0]))(lambda: fill((1,)))
    pl.when(jnp.logical_not(live[0] | live[1]))(lambda: fill(()))

    @pl.when((info_ref[0] == 1) & (info_ref[1] == odd))
    def _():
        i = lax.broadcasted_iota(jnp.int32, (T, T), 0)
        j = lax.broadcasted_iota(jnp.int32, (T, T), 1)
        extra = jnp.where(i == j, diag_ref[0], 0.0)
        for lane in range(2):
            tile[lane, pl.ds(k, T, stride=G), :] += extra[:, lane * L : lane * L + L]

    for m in range(8):
        for lane in range(2):
            out_ref[0, pl.ds(m * 32, 32), :, pl.ds(lane * L, L)] = (
                tile[lane, pl.ds(m * 256, 256), :].reshape(32, G, L).astype(BF)
            )


def assemble(rows, cols, info, recv, v, pcol, diag):
    whole = pl.BlockSpec((G, T, T), lambda k, o, *_: (0, 0, 0))
    recv, v, pcol = (pltpu.with_memory_space_constraint(x, pltpu.VMEM) for x in (recv, v, pcol))
    return pl.pallas_call(
        assemble_kernel,
        out_shape=jax.ShapeDtypeStruct((2 * G, T, G, T), BF),
        grid_spec=pltpu.PrefetchScalarGridSpec(
            num_scalar_prefetch=3,
            grid=(G, 2),
            in_specs=[
                pl.BlockSpec(memory_space=pltpu.VMEM),
                whole,
                pl.BlockSpec((1, T, T), lambda k, o, *_: (2 * k + o, 0, 0)),
                pl.BlockSpec((1, 1, T), lambda k, o, *_: (2 * k + o, 0, 0)),
            ],
            out_specs=pl.BlockSpec((1, T, G, T), lambda k, o, *_: (2 * k + o, 0, 0, 0)),
            scratch_shapes=[pltpu.VMEM((2, T * G, L), F32)],
        ),
        compiler_params=pltpu.CompilerParams(vmem_limit_bytes=12 << 20),
        name="assemble",
    )(rows, cols, info, recv, v, pcol, diag)


def shards(
    child_block,
    child_row,
    child_col,
    child_pivot_inv,
    child_map,
    parent_row,
    parent_col,
    parent_pivot_inv,
    parent_diag,
):
    h = lax.axis_index("half")
    r = lax.axis_index("row")
    c = lax.axis_index("col")
    steps = jnp.arange(G, dtype=jnp.int32)
    shift = child_map.reshape(2, G, G)[:, :, 0] - 2 * G * steps[None, :]
    source = jnp.sum(
        jnp.where(shift[:, None, :] == steps[None, :, None], steps[None, None, :], 0), axis=2
    ).astype(jnp.int32)
    q = lax.dynamic_index_in_dim(source, h, 0, keepdims=False)

    def ordered(x):
        x = x.reshape(x.shape[1], G, T)
        return jnp.swapaxes(jnp.take(x, q, axis=1), 0, 1)

    crow = ordered(child_row)
    ccol = ordered(child_col)
    prow = jnp.swapaxes(parent_row.reshape(-1, G, T), 0, 1)
    pcol = jnp.swapaxes(parent_col.reshape(-1, 2 * G, T), 0, 1)
    cinv = jnp.swapaxes(child_pivot_inv.reshape(4, 2, 32, T), 0, 1).reshape(T, T)
    pinv = jnp.transpose(parent_pivot_inv.reshape(2, 4, 2, 16, T), (2, 0, 1, 3, 4)).reshape(T, T)
    recv, v, pcols = exchange(
        q, child_block.reshape(G, T, G, T), crow, ccol, prow, pcol, cinv, pinv
    )
    rows = ((r - shift) % G).reshape(-1)
    cols = ((c - shift) % G).reshape(-1)
    carry = (shift > r).astype(jnp.int32).reshape(-1)
    head = jnp.stack([(r == c).astype(jnp.int32), h.astype(jnp.int32)])
    info = jnp.concatenate([head, carry])
    out = assemble(rows, cols, info, recv, v, pcols, parent_diag)
    return out.reshape(2 * G, 1, T, G, 1, T)


def solution(mesh):
    return jax.shard_map(
        shards,
        mesh=mesh,
        in_specs=(
            P("half", None, "row", None, None, "col", None),
            P("half", "row", None, "col", None),
            P("half", "col", None, "row", None),
            P("half", None, None),
            P(),
            P("row", None, ("half", "col"), None),
            P(("half", "col"), None, "row", None),
            P(),
            P(None, "row", None),
        ),
        out_specs=P(None, "row", None, None, ("half", "col"), None),
        check_vma=False,
    )
```

```python
import functools

import jax
import jax.numpy as jnp
from jax import lax
from jax.experimental import pallas as pl
from jax.experimental.pallas import tpu as pltpu
from jax.sharding import PartitionSpec as P

MESH = pl.DeviceIdType.MESH
T = 256
L = 128
G = 8
BF = jnp.bfloat16
F32 = jnp.float32

RELAYED = {
    (0, 0): (2, 6, 7),
    (0, 1): (4, 6, 7),
    (0, 2): (0, 7),
    (0, 3): (1, 4, 7),
    (0, 5): (3,),
    (0, 6): (0, 3),
    (0, 7): (0,),
    (1, 0): (7,),
    (1, 1): (5, 7),
    (1, 2): (6,),
    (1, 3): (5,),
    (1, 4): (0, 1, 6),
    (1, 6): (1, 3),
    (1, 7): (0, 1, 2),
}
RELAYS = {}
for (_h, _c), _cols in RELAYED.items():
    for _v in _cols:
        RELAYS.setdefault((1 if _v < _c else 0, _c), []).append((_h, _v))
RELAY_SLOTS = max(len(v) for v in RELAYS.values())


def relay_route(h, c, target):
    relayed = h < 0
    slot = 0 * c
    for (hh, cc), cols in RELAYED.items():
        for v in cols:
            hit = (h == hh) & (c == cc) & (target == v)
            relayed = relayed | hit
            k = RELAYS[(1 if v < cc else 0, cc)].index((hh, v))
            if k:
                slot = jnp.where(hit, k, slot)
    return relayed, slot


def turn_of(i):
    return 5 * i % G, (2 * (i // G) + i // (4 * G) + i) % G


def exchange_kernel(
    q_ref,
    block_hbm,
    crow_in,
    ccol_in,
    prow_in,
    pcol_in,
    cinv_in,
    pinv_in,
    recv_hbm,
    v_ref,
    pcol_hbm,
    stage,
    tile,
    plain,
    rowg,
    colg,
    colt,
    w,
    sbuf,
    lbuf,
    prowg,
    zeros,
    crow_ref,
    ccol_ref,
    prow_ref,
    pcol_ref,
    cinv_ref,
    pinv_ref,
    natural,
    stage_sem,
    row_sem,
    col_sem,
    prow_sem,
    pcol_sem,
    ssem,
    rsem,
    lsem,
    fsem,
):
    h = lax.axis_index("half")
    r = lax.axis_index("row")
    c = lax.axis_index("col")
    slot_me = h * G + c

    def remote(src, dst, send, recv, dev):
        return pltpu.make_async_remote_copy(
            src_ref=src,
            dst_ref=dst,
            send_sem=send,
            recv_sem=recv,
            device_id=dev,
            device_id_type=MESH,
        )

    def fetch(k, s):
        return pltpu.make_async_copy(block_hbm.at[k], stage.at[s], stage_sem.at[s])

    fetch(0, 0).start()

    barrier = pltpu.get_barrier_semaphore()
    me = h * 64 + r * 8 + c

    def greet(i, _):
        @pl.when(i != me)
        def _():
            pl.semaphore_signal(
                barrier,
                inc=1,
                device_id=(i // 64, (i // 8) % 8, i % 8),
                device_id_type=MESH,
            )

        return 0

    lax.fori_loop(0, 128, greet, 0)

    def blocks(panel, count, put):
        deep = panel.shape[0]
        x = panel[...].astype(F32).reshape(deep * count, T)
        for lane in range(2):
            tile[lane, pl.ds(0, deep * count), :] = x[:, lane * L : lane * L + L]
        for k in range(count):
            for lane in range(2):
                put[k, pl.ds(0, deep), pl.ds(lane * L, L)] = tile[
                    lane, pl.ds(k, deep, stride=count), :
                ].astype(BF)

    blocks(crow_in, G, natural)
    for k in range(G):
        crow_ref[k] = natural[q_ref[k]]
    blocks(ccol_in, G, natural)
    for k in range(G):
        ccol_ref[k] = natural[q_ref[k]]
    blocks(prow_in, G, prow_ref)
    blocks(pcol_in, 2 * G, pcol_ref)
    for x in range(4):
        for core in range(2):
            cinv_ref[pl.ds((core * 4 + x) * 32, 32), :] = cinv_in[pl.ds((x * 2 + core) * 32, 32), :]
            for half in range(2):
                pinv_ref[pl.ds((core * 8 + half * 4 + x) * 16, 16), :] = pinv_in[
                    pl.ds((half * 8 + x * 2 + core) * 16, 16), :
                ]
    pl.semaphore_wait(barrier, 127)

    other = (1 - h, r, c)
    pair = (h, (r + G // 2) % G, c)
    twin = (h, r, c + 1 - 2 * (c % 2))
    row_part = pl.ds(pl.multiple_of(r * 32, 32), 32)
    pair_part = pl.ds(pl.multiple_of((r + G // 2) % G * 32, 32), 32)

    def rows_out(panel, whole, sems):
        remote(panel, whole.at[:, row_part, :], sems.at[0], sems.at[2], pair).start()
        for t in range(1, 4):
            to = (h, r // 4 * 4 + (r + t) % 4, c)
            remote(panel, whole.at[:, row_part, :], sems.at[0], sems.at[3], to).start()
        pltpu.make_async_copy(panel, whole.at[:, row_part, :], sems.at[3]).start()

    def rows_on(whole, sems):
        part = whole.at[:, pair_part, :]
        remote(part, part, sems.at[0], sems.at[2], pair).wait_recv()
        for t in range(1, 4):
            to = (h, r // 4 * 4 + (r + t) % 4, c)
            remote(part, part, sems.at[1], sems.at[4], to).start()

    def rows_in(whole, sems):
        four, three = whole.at[pl.ds(0, 4)], whole.at[pl.ds(0, 3)]
        remote(four, four, sems.at[0], sems.at[3], pair).wait_recv()
        remote(three, three, sems.at[0], sems.at[4], pair).wait_recv()

    def rows_left(whole, sems):
        four, three = whole.at[pl.ds(0, 4)], whole.at[pl.ds(0, 3)]
        remote(four, four, sems.at[0], sems.at[3], pair).wait_send()
        remote(three, three, sems.at[1], sems.at[4], pair).wait_send()

    ccol_part = pl.ds(pl.multiple_of(c % 2 * 128 + c // 2 * 32, 32), 32)
    ccol_core = pl.ds(pl.multiple_of(c % 2 * 128, 128), 128)
    pcol_part = pl.ds(pl.multiple_of(c % 2 * 128 + h * 64 + c // 2 * 16, 16), 16)
    pcol_over = pl.ds(pl.multiple_of(c % 2 * 128 + (1 - h) * 64 + c // 2 * 16, 16), 16)
    pcol_core = pl.ds(pl.multiple_of(c % 2 * 128, 128), 128)

    rows_out(crow_ref, rowg, row_sem)
    for t in range(1, 4):
        to = (h, r, (c + 2 * t) % G)
        remote(ccol_ref, colg.at[:, ccol_part, :], col_sem.at[0], col_sem.at[2], to).start()
    pltpu.make_async_copy(ccol_ref, colg.at[:, ccol_part, :], col_sem.at[2]).start()
    rows_on(rowg, row_sem)
    remote(pcol_ref, pcol_hbm.at[:, pcol_part, :], pcol_sem.at[0], pcol_sem.at[3], other).start()
    rows_out(prow_ref, prowg, prow_sem)
    for t in range(1, 4):
        to = (h, r, (c + 2 * t) % G)
        remote(pcol_ref, pcol_hbm.at[:, pcol_part, :], pcol_sem.at[0], pcol_sem.at[4], to).start()
    pltpu.make_async_copy(pcol_ref, pcol_hbm.at[:, pcol_part, :], pcol_sem.at[4]).start()

    def split(k, _):
        s = k % 2

        @pl.when(k + 1 < G)
        def _():
            fetch(k + 1, 1 - s).start()

        fetch(k, s).wait()

        def widen(m, _):
            x = stage[s, pl.ds(pl.multiple_of(m * 32, 32), 32)]
            x = x.astype(F32).reshape(256, T)
            for lane in range(2):
                tile[lane, pl.ds(pl.multiple_of(m * 256, 256), 256), :] = x[:, lane * L : lane * L + L]
            return 0

        lax.fori_loop(0, 8, widen, 0)
        for kk in range(G):
            for lane in range(2):
                plain[k * G + kk, :, pl.ds(lane * L, L)] = tile[
                    lane, pl.ds(kk, T, stride=G), :
                ].astype(BF)
        return 0

    lax.fori_loop(0, G, split, 0)

    zeros[...] = jnp.zeros_like(zeros)
    half_part = colg.at[:, ccol_core, :]
    remote(half_part, half_part, col_sem.at[0], col_sem.at[2], twin).wait_recv()
    remote(half_part, half_part, col_sem.at[1], col_sem.at[3], twin).start()
    remote(half_part, half_part, col_sem.at[1], col_sem.at[3], twin).wait_recv()

    def turn(k, _):
        colt[k] = colg[k].T
        return 0

    lax.fori_loop(0, G, turn, 0)
    rows_in(rowg, row_sem)

    def scale(k, _):
        w[k] = jnp.dot(cinv_ref[...], rowg[k], preferred_element_type=F32).astype(BF)
        return 0

    lax.fori_loop(0, G, scale, 0)

    def block(i, _):
        d, dd = turn_of(i % (G * G))
        s = d * G + dd
        to = c + dd
        th, tr, tc = to // G, (r + d) % G, to % G
        relayed, slot = relay_route(h, c, tc)
        relayed = relayed & ((th != h) | (tr != r))
        here = (d == 0) & (to == slot_me)
        sent = jnp.where(s == 0, G, d)

        def make():
            update = jnp.dot(colt[d], w[dd], preferred_element_type=F32)
            sbuf[s] = (plain[q_ref[d] * G + q_ref[dd]].astype(F32) - update).astype(BF)

        @pl.when(relayed & (i < G * G))
        def _():
            make()
            remote(
                sbuf.at[s],
                lbuf.at[slot * G + r],
                ssem.at[sent],
                lsem.at[slot * G + r],
                (th, tr, c),
            ).start()

        @pl.when(jnp.logical_not(relayed) & (i >= G * G))
        def _():
            make()

            @pl.when(jnp.logical_not(here))
            def _():
                remote(
                    sbuf.at[s],
                    recv_hbm.at[h, r, c],
                    ssem.at[sent],
                    rsem.at[h * G + c],
                    (th, tr, tc),
                ).start()

            @pl.when(here)
            def _():
                pltpu.make_async_copy(sbuf.at[s], recv_hbm.at[h, r, c], rsem.at[h * G + c]).start()

        return 0

    lax.fori_loop(0, G * G, block, 0)
    rows_on(prowg, prow_sem)
    part = pcol_hbm.at[:, pcol_over, :]
    remote(part, part, pcol_sem.at[0], pcol_sem.at[3], other).wait_recv()
    for t in range(1, 4):
        to = (h, r, (c + 2 * t) % G)
        remote(part, part, pcol_sem.at[1], pcol_sem.at[5], to).start()

    lax.fori_loop(G * G, 2 * G * G, block, 0)

    for hs in range(2):
        for cs in range(G):

            @pl.when((slot_me - cs < 0) | (slot_me - cs >= G))
            def _(hs=hs, cs=cs):
                pltpu.make_async_copy(zeros, recv_hbm.at[hs, :, cs], rsem.at[hs * G + cs]).start()

    for (rh, rc), passing in RELAYS.items():

        @pl.when((h == rh) & (c == rc))
        def _(rh=rh, rc=rc, passing=passing):
            def forward(i, _):
                d, dd = turn_of(i)
                frm = (r - d + G) % G
                for slot, (hs, tc) in enumerate(passing):
                    due = dd == (tc - rc) % G
                    if hs == rh:
                        due = due & (d != 0)

                    @pl.when(due)
                    def _(slot=slot, hs=hs, tc=tc):
                        buf = lbuf.at[slot * G + frm]
                        remote(
                            buf, buf, fsem.at[slot], lsem.at[slot * G + frm], (1 - h, r, c)
                        ).wait_recv()
                        remote(
                            buf,
                            recv_hbm.at[hs, frm, c],
                            fsem.at[slot],
                            rsem.at[hs * G + c],
                            (h, r, tc),
                        ).start()

                return 0

            lax.fori_loop(0, G * G, forward, 0)

    four = pcol_hbm.at[pl.ds(0, 4)]
    three = pcol_hbm.at[pl.ds(0, 3)]
    remote(four, four, pcol_sem.at[0], pcol_sem.at[4], other).wait_recv()
    remote(three, three, pcol_sem.at[0], pcol_sem.at[5], other).wait_recv()
    part = pcol_hbm.at[:, pcol_core, :]
    remote(part, part, pcol_sem.at[2], pcol_sem.at[6], twin).start()

    rows_in(prowg, prow_sem)

    def pscale(k, _):
        v_ref[k] = -jnp.dot(pinv_ref[...], prowg[k], preferred_element_type=F32).astype(BF)
        return 0

    lax.fori_loop(0, G, pscale, 0)

    rows_left(rowg, row_sem)
    rows_left(prowg, prow_sem)
    quarter = colg.at[:, pl.ds(0, 96), :]
    remote(quarter, quarter, col_sem.at[0], col_sem.at[2], twin).wait_send()
    remote(half_part, half_part, col_sem.at[1], col_sem.at[3], twin).wait_send()
    remote(four, four, pcol_sem.at[0], pcol_sem.at[3], twin).wait_send()
    remote(three, three, pcol_sem.at[1], pcol_sem.at[3], twin).wait_send()
    part = pcol_hbm.at[:, pcol_core, :]
    remote(part, part, pcol_sem.at[2], pcol_sem.at[6], twin).wait_send()
    remote(part, part, pcol_sem.at[2], pcol_sem.at[6], twin).wait_recv()

    for (rh, rc), passing in RELAYS.items():

        @pl.when((h == rh) & (c == rc))
        def _(rh=rh, passing=passing):
            for slot, (hs, _tc) in enumerate(passing):
                part = lbuf.at[pl.ds(0, G - 1 if hs == rh else G)]
                remote(part, part, fsem.at[slot], lsem.at[0], other).wait_send()

    part = sbuf.at[pl.ds(0, G - 1)]
    remote(part, part, ssem.at[0], rsem.at[0], other).wait_send()

    @pl.when(h == 1)
    def _():
        one = sbuf.at[pl.ds(0, 1)]
        remote(one, one, ssem.at[G], rsem.at[0], other).wait_send()

    for d in range(1, G):
        part = sbuf.at[pl.ds(0, G)]
        remote(part, part, ssem.at[d], rsem.at[0], other).wait_send()

    for hs in range(2):
        for cs in range(G):
            dst = recv_hbm.at[hs, :, cs]
            remote(sbuf.at[pl.ds(0, G)], dst, ssem.at[0], rsem.at[hs * G + cs], other).wait_recv()


def exchange(q, block, crow, ccol, prow, pcol, cinv, pinv):
    any_space = pl.BlockSpec(memory_space=pl.ANY)
    vmem = pl.BlockSpec(memory_space=pltpu.VMEM)
    smem = pl.BlockSpec(memory_space=pltpu.SMEM)
    dma = pltpu.SemaphoreType.DMA
    return pl.pallas_call(
        exchange_kernel,
        out_shape=(
            pltpu.VMEM((2, G, G, T, T), BF),
            pltpu.VMEM((G, T, T), BF),
            pltpu.VMEM((2 * G, T, T), BF),
        ),
        in_specs=[smem, any_space] + [vmem] * 6,
        out_specs=(any_space, vmem, any_space),
        scratch_shapes=[
            pltpu.VMEM((2, T, G, T), BF),
            pltpu.VMEM((2, T * G, L), F32),
            pltpu.VMEM((G * G, T, T), BF),
            pltpu.VMEM((G, T, T), BF),
            pltpu.VMEM((G, T, T), BF),
            pltpu.VMEM((G, T, T), BF),
            pltpu.VMEM((G, T, T), BF),
            pltpu.VMEM((G * G, T, T), BF),
            pltpu.VMEM((RELAY_SLOTS * G, T, T), BF),
            pltpu.VMEM((G, T, T), BF),
            pltpu.VMEM((G, T, T), BF),
            pltpu.VMEM((G, 32, T), BF),
            pltpu.VMEM((G, 32, T), BF),
            pltpu.VMEM((G, 32, T), BF),
            pltpu.VMEM((2 * G, 16, T), BF),
            pltpu.VMEM((T, T), BF),
            pltpu.VMEM((T, T), BF),
            pltpu.VMEM((G, 32, T), BF),
            dma((2,)),
            dma((5,)),
            dma((4,)),
            dma((5,)),
            dma((7,)),
            dma((G + 1,)),
            dma((2 * G,)),
            dma((RELAY_SLOTS * G,)),
            dma((RELAY_SLOTS,)),
        ],
        compiler_params=pltpu.CompilerParams(
            collective_id=0, has_side_effects=True, vmem_limit_bytes=37 << 20
        ),
        name="exchange",
    )(q, block, crow, ccol, prow, pcol, cinv, pinv)


OUT_SLOTS = 4


def assemble_kernel(
    rows_ref, cols_ref, info_ref, recv_ref, v_ref, pcol_ref, diag_ref, out_hbm, tile, done, sem
):
    a = pl.program_id(0)
    k = a // 2
    odd = a % 2
    slot = a % OUT_SLOTS
    live = [info_ref[2 + hs * G + k] == odd for hs in range(2)]

    def put(s, row):
        return pltpu.make_async_copy(done.at[s], out_hbm.at[row], sem.at[s])

    def fill(parts):
        pc = pcol_ref[a].T
        for b in range(G):
            acc = jnp.dot(pc, v_ref[b], preferred_element_type=F32)
            for hs in parts:
                acc = acc + recv_ref[hs, rows_ref[hs * G + k], cols_ref[hs * G + b]].astype(F32)
            for lane in range(2):
                tile[lane, pl.ds(b, T, stride=G), :] = acc[:, lane * L : lane * L + L]

    pl.when(live[0] & live[1])(lambda: fill((0, 1)))
    pl.when(live[0] & jnp.logical_not(live[1]))(lambda: fill((0,)))
    pl.when(live[1] & jnp.logical_not(live[0]))(lambda: fill((1,)))
    pl.when(jnp.logical_not(live[0] | live[1]))(lambda: fill(()))

    @pl.when((info_ref[0] == 1) & (info_ref[1] == odd))
    def _():
        i = lax.broadcasted_iota(jnp.int32, (T, T), 0)
        j = lax.broadcasted_iota(jnp.int32, (T, T), 1)
        extra = jnp.where(i == j, diag_ref[a], 0.0)
        for lane in range(2):
            tile[lane, pl.ds(k, T, stride=G), :] += extra[:, lane * L : lane * L + L]

    @pl.when(a >= OUT_SLOTS)
    def _():
        put(slot, a).wait()

    for m in range(8):
        for lane in range(2):
            done[slot, pl.ds(m * 32, 32), :, pl.ds(lane * L, L)] = (
                tile[lane, pl.ds(m * 256, 256), :].reshape(32, G, L).astype(BF)
            )
    put(slot, a).start()

    @pl.when(a == 2 * G - 1)
    def _():
        for s in range(OUT_SLOTS):
            put(s, a).wait()


def assemble(rows, cols, info, recv, v, pcol, diag):
    recv, v, pcol = (pltpu.with_memory_space_constraint(x, pltpu.VMEM) for x in (recv, v, pcol))
    vmem = pl.BlockSpec(memory_space=pltpu.VMEM)
    return pl.pallas_call(
        assemble_kernel,
        out_shape=jax.ShapeDtypeStruct((2 * G, T, G, T), BF),
        grid_spec=pltpu.PrefetchScalarGridSpec(
            num_scalar_prefetch=3,
            grid=(2 * G,),
            in_specs=[vmem] * 4,
            out_specs=pl.BlockSpec(memory_space=pl.ANY),
            scratch_shapes=[
                pltpu.VMEM((2, T * G, L), F32),
                pltpu.VMEM((OUT_SLOTS, T, G, T), BF),
                pltpu.SemaphoreType.DMA((OUT_SLOTS,)),
            ],
        ),
        compiler_params=pltpu.CompilerParams(vmem_limit_bytes=12 << 20),
        name="assemble",
    )(rows, cols, info, recv, v, pcol, diag)


def shards(
    child_block,
    child_row,
    child_col,
    child_pivot_inv,
    child_map,
    parent_row,
    parent_col,
    parent_pivot_inv,
    parent_diag,
):
    h = lax.axis_index("half")
    r = lax.axis_index("row")
    c = lax.axis_index("col")
    steps = jnp.arange(G, dtype=jnp.int32)
    shift = child_map.reshape(2, G, G)[:, :, 0] - 2 * G * steps[None, :]
    source = jnp.sum(
        jnp.where(shift[:, None, :] == steps[None, :, None], steps[None, None, :], 0), axis=2
    ).astype(jnp.int32)
    q = lax.dynamic_index_in_dim(source, h, 0, keepdims=False)

    recv, v, pcols = exchange(
        q,
        child_block.reshape(G, T, G, T),
        child_row.reshape(-1, G, T),
        child_col.reshape(-1, G, T),
        parent_row.reshape(-1, G, T),
        parent_col.reshape(-1, 2 * G, T),
        child_pivot_inv[0],
        parent_pivot_inv,
    )
    rows = ((r - shift) % G).reshape(-1)
    cols = ((c - shift) % G).reshape(-1)
    carry = (shift > r).astype(jnp.int32).reshape(-1)
    head = jnp.stack([(r == c).astype(jnp.int32), h.astype(jnp.int32)])
    info = jnp.concatenate([head, carry])
    out = assemble(rows, cols, info, recv, v, pcols, parent_diag)
    return out.reshape(2 * G, 1, T, G, 1, T)


def solution(mesh):
    return jax.shard_map(
        shards,
        mesh=mesh,
        in_specs=(
            P("half", None, "row", None, None, "col", None),
            P("half", "row", None, "col", None),
            P("half", "col", None, "row", None),
            P("half", None, None),
            P(),
            P("row", None, ("half", "col"), None),
            P(("half", "col"), None, "row", None),
            P(),
            P(None, "row", None),
        ),
        out_specs=P(None, "row", None, None, ("half", "col"), None),
        check_vma=False,
    )
```

```python
import functools

import jax
import jax.numpy as jnp
from jax import lax
from jax.experimental import pallas as pl
from jax.experimental.pallas import tpu as pltpu
from jax.sharding import PartitionSpec as P

MESH = pl.DeviceIdType.MESH
T = 256
L = 128
G = 8
BF = jnp.bfloat16
F32 = jnp.float32

RELAYED = {
    (0, 0): (2, 6, 7),
    (0, 1): (4, 6, 7),
    (0, 2): (0, 7),
    (0, 3): (1, 4, 7),
    (0, 5): (3,),
    (0, 6): (0, 3),
    (0, 7): (0,),
    (1, 0): (7,),
    (1, 1): (5, 7),
    (1, 2): (6,),
    (1, 3): (5,),
    (1, 4): (0, 1, 6),
    (1, 6): (1, 3),
    (1, 7): (0, 1, 2),
}
RELAYS = {}
for (_h, _c), _cols in RELAYED.items():
    for _v in _cols:
        RELAYS.setdefault((1 if _v < _c else 0, _c), []).append((_h, _v))
RELAY_SLOTS = max(len(v) for v in RELAYS.values())


def relay_route(h, c, target):
    relayed = h < 0
    slot = 0 * c
    for (hh, cc), cols in RELAYED.items():
        for v in cols:
            hit = (h == hh) & (c == cc) & (target == v)
            relayed = relayed | hit
            k = RELAYS[(1 if v < cc else 0, cc)].index((hh, v))
            if k:
                slot = jnp.where(hit, k, slot)
    return relayed, slot


def turn_of(i):
    return 5 * i % G, (2 * (i // G) + i // (4 * G) + i) % G


def exchange_kernel(
    map_ref,
    block_hbm,
    crow_in,
    ccol_in,
    prow_in,
    pcol_in,
    cinv_in,
    pinv_in,
    recv_hbm,
    v_ref,
    pcol_hbm,
    stage,
    tile,
    plain,
    rowg,
    colg,
    colt,
    w,
    sbuf,
    lbuf,
    prowg,
    zeros,
    crow_ref,
    ccol_ref,
    prow_ref,
    pcol_ref,
    cinv_ref,
    pinv_ref,
    natural,
    q_ref,
    stage_sem,
    row_sem,
    col_sem,
    prow_sem,
    pcol_sem,
    ssem,
    rsem,
    lsem,
    fsem,
):
    h = lax.axis_index("half")
    r = lax.axis_index("row")
    c = lax.axis_index("col")
    slot_me = h * G + c

    def remote(src, dst, send, recv, dev):
        return pltpu.make_async_remote_copy(
            src_ref=src,
            dst_ref=dst,
            send_sem=send,
            recv_sem=recv,
            device_id=dev,
            device_id_type=MESH,
        )

    def fetch(k, s):
        return pltpu.make_async_copy(block_hbm.at[k], stage.at[s], stage_sem.at[s])

    fetch(0, 0).start()

    barrier = pltpu.get_barrier_semaphore()
    me = h * 64 + r * 8 + c

    def greet(i, _):
        @pl.when(i != me)
        def _():
            pl.semaphore_signal(
                barrier,
                inc=1,
                device_id=(i // 64, (i // 8) % 8, i % 8),
                device_id_type=MESH,
            )

        return 0

    lax.fori_loop(0, 128, greet, 0)

    moves = [map_ref[h, G * k] - 2 * G * k for k in range(G)]
    for d in range(G):
        found = jnp.int32(0)
        for k in range(G):
            found = found + jnp.where(moves[k] == d, k, 0)
        q_ref[d] = found

    def blocks(panel, count, put):
        deep = panel.shape[0]
        x = panel[...].astype(F32).reshape(deep * count, T)
        for lane in range(2):
            tile[lane, pl.ds(0, deep * count), :] = x[:, lane * L : lane * L + L]
        for k in range(count):
            for lane in range(2):
                put[k, pl.ds(0, deep), pl.ds(lane * L, L)] = tile[
                    lane, pl.ds(k, deep, stride=count), :
                ].astype(BF)

    blocks(crow_in, G, natural)
    for k in range(G):
        crow_ref[k] = natural[q_ref[k]]
    blocks(ccol_in, G, natural)
    for k in range(G):
        ccol_ref[k] = natural[q_ref[k]]
    blocks(prow_in, G, prow_ref)
    blocks(pcol_in, 2 * G, pcol_ref)
    for x in range(4):
        for core in range(2):
            cinv_ref[pl.ds((core * 4 + x) * 32, 32), :] = cinv_in[pl.ds((x * 2 + core) * 32, 32), :]
            for half in range(2):
                pinv_ref[pl.ds((core * 8 + half * 4 + x) * 16, 16), :] = pinv_in[
                    pl.ds((half * 8 + x * 2 + core) * 16, 16), :
                ]
    pl.semaphore_wait(barrier, 127)

    other = (1 - h, r, c)
    pair = (h, (r + G // 2) % G, c)
    twin = (h, r, c + 1 - 2 * (c % 2))
    row_part = pl.ds(pl.multiple_of(r * 32, 32), 32)
    pair_part = pl.ds(pl.multiple_of((r + G // 2) % G * 32, 32), 32)

    def rows_out(panel, whole, sems):
        remote(panel, whole.at[:, row_part, :], sems.at[0], sems.at[2], pair).start()
        for t in range(1, 4):
            to = (h, r // 4 * 4 + (r + t) % 4, c)
            remote(panel, whole.at[:, row_part, :], sems.at[0], sems.at[3], to).start()
        pltpu.make_async_copy(panel, whole.at[:, row_part, :], sems.at[3]).start()

    def rows_on(whole, sems):
        part = whole.at[:, pair_part, :]
        remote(part, part, sems.at[0], sems.at[2], pair).wait_recv()
        for t in range(1, 4):
            to = (h, r // 4 * 4 + (r + t) % 4, c)
            remote(part, part, sems.at[1], sems.at[4], to).start()

    def rows_in(whole, sems):
        four, three = whole.at[pl.ds(0, 4)], whole.at[pl.ds(0, 3)]
        remote(four, four, sems.at[0], sems.at[3], pair).wait_recv()
        remote(three, three, sems.at[0], sems.at[4], pair).wait_recv()

    def rows_left(whole, sems):
        four, three = whole.at[pl.ds(0, 4)], whole.at[pl.ds(0, 3)]
        remote(four, four, sems.at[0], sems.at[3], pair).wait_send()
        remote(three, three, sems.at[1], sems.at[4], pair).wait_send()

    ccol_part = pl.ds(pl.multiple_of(c % 2 * 128 + c // 2 * 32, 32), 32)
    ccol_core = pl.ds(pl.multiple_of(c % 2 * 128, 128), 128)
    pcol_part = pl.ds(pl.multiple_of(c % 2 * 128 + h * 64 + c // 2 * 16, 16), 16)
    pcol_over = pl.ds(pl.multiple_of(c % 2 * 128 + (1 - h) * 64 + c // 2 * 16, 16), 16)
    pcol_core = pl.ds(pl.multiple_of(c % 2 * 128, 128), 128)

    rows_out(crow_ref, rowg, row_sem)
    for t in range(1, 4):
        to = (h, r, (c + 2 * t) % G)
        remote(ccol_ref, colg.at[:, ccol_part, :], col_sem.at[0], col_sem.at[2], to).start()
    pltpu.make_async_copy(ccol_ref, colg.at[:, ccol_part, :], col_sem.at[2]).start()
    rows_on(rowg, row_sem)
    remote(pcol_ref, pcol_hbm.at[:, pcol_part, :], pcol_sem.at[0], pcol_sem.at[3], other).start()
    rows_out(prow_ref, prowg, prow_sem)
    for t in range(1, 4):
        to = (h, r, (c + 2 * t) % G)
        remote(pcol_ref, pcol_hbm.at[:, pcol_part, :], pcol_sem.at[0], pcol_sem.at[4], to).start()
    pltpu.make_async_copy(pcol_ref, pcol_hbm.at[:, pcol_part, :], pcol_sem.at[4]).start()

    def split(k, _):
        s = k % 2

        @pl.when(k + 1 < G)
        def _():
            fetch(k + 1, 1 - s).start()

        fetch(k, s).wait()

        def widen(m, _):
            x = stage[s, pl.ds(pl.multiple_of(m * 32, 32), 32)]
            x = x.astype(F32).reshape(256, T)
            for lane in range(2):
                tile[lane, pl.ds(pl.multiple_of(m * 256, 256), 256), :] = x[:, lane * L : lane * L + L]
            return 0

        lax.fori_loop(0, 8, widen, 0)
        for kk in range(G):
            for lane in range(2):
                plain[k * G + kk, :, pl.ds(lane * L, L)] = tile[
                    lane, pl.ds(kk, T, stride=G), :
                ].astype(BF)
        return 0

    lax.fori_loop(0, G, split, 0)

    zeros[...] = jnp.zeros_like(zeros)
    half_part = colg.at[:, ccol_core, :]
    remote(half_part, half_part, col_sem.at[0], col_sem.at[2], twin).wait_recv()
    remote(half_part, half_part, col_sem.at[1], col_sem.at[3], twin).start()
    remote(half_part, half_part, col_sem.at[1], col_sem.at[3], twin).wait_recv()

    def turn(k, _):
        colt[k] = colg[k].T
        return 0

    lax.fori_loop(0, G, turn, 0)
    rows_in(rowg, row_sem)

    def scale(k, _):
        w[k] = jnp.dot(cinv_ref[...], rowg[k], preferred_element_type=F32).astype(BF)
        return 0

    lax.fori_loop(0, G, scale, 0)

    def block(i, _):
        d, dd = turn_of(i % (G * G))
        s = d * G + dd
        to = c + dd
        th, tr, tc = to // G, (r + d) % G, to % G
        relayed, slot = relay_route(h, c, tc)
        relayed = relayed & ((th != h) | (tr != r))
        here = (d == 0) & (to == slot_me)
        sent = jnp.where(s == 0, G, d)

        def make():
            update = jnp.dot(colt[d], w[dd], preferred_element_type=F32)
            sbuf[s] = (plain[q_ref[d] * G + q_ref[dd]].astype(F32) - update).astype(BF)

        @pl.when(relayed & (i < G * G))
        def _():
            make()
            remote(
                sbuf.at[s],
                lbuf.at[slot * G + r],
                ssem.at[sent],
                lsem.at[slot * G + r],
                (th, tr, c),
            ).start()

        @pl.when(jnp.logical_not(relayed) & (i >= G * G))
        def _():
            make()

            @pl.when(jnp.logical_not(here))
            def _():
                remote(
                    sbuf.at[s],
                    recv_hbm.at[h, r, c],
                    ssem.at[sent],
                    rsem.at[h * G + c],
                    (th, tr, tc),
                ).start()

            @pl.when(here)
            def _():
                pltpu.make_async_copy(sbuf.at[s], recv_hbm.at[h, r, c], rsem.at[h * G + c]).start()

        return 0

    lax.fori_loop(0, G * G, block, 0)
    rows_on(prowg, prow_sem)
    part = pcol_hbm.at[:, pcol_over, :]
    remote(part, part, pcol_sem.at[0], pcol_sem.at[3], other).wait_recv()
    for t in range(1, 4):
        to = (h, r, (c + 2 * t) % G)
        remote(part, part, pcol_sem.at[1], pcol_sem.at[5], to).start()

    lax.fori_loop(G * G, 2 * G * G, block, 0)

    for hs in range(2):
        for cs in range(G):

            @pl.when((slot_me - cs < 0) | (slot_me - cs >= G))
            def _(hs=hs, cs=cs):
                pltpu.make_async_copy(zeros, recv_hbm.at[hs, :, cs], rsem.at[hs * G + cs]).start()

    for (rh, rc), passing in RELAYS.items():

        @pl.when((h == rh) & (c == rc))
        def _(rh=rh, rc=rc, passing=passing):
            def forward(i, _):
                d, dd = turn_of(i)
                frm = (r - d + G) % G
                for slot, (hs, tc) in enumerate(passing):
                    due = dd == (tc - rc) % G
                    if hs == rh:
                        due = due & (d != 0)

                    @pl.when(due)
                    def _(slot=slot, hs=hs, tc=tc):
                        buf = lbuf.at[slot * G + frm]
                        remote(
                            buf, buf, fsem.at[slot], lsem.at[slot * G + frm], (1 - h, r, c)
                        ).wait_recv()
                        remote(
                            buf,
                            recv_hbm.at[hs, frm, c],
                            fsem.at[slot],
                            rsem.at[hs * G + c],
                            (h, r, tc),
                        ).start()

                return 0

            lax.fori_loop(0, G * G, forward, 0)

    four = pcol_hbm.at[pl.ds(0, 4)]
    three = pcol_hbm.at[pl.ds(0, 3)]
    remote(four, four, pcol_sem.at[0], pcol_sem.at[4], other).wait_recv()
    remote(three, three, pcol_sem.at[0], pcol_sem.at[5], other).wait_recv()
    part = pcol_hbm.at[:, pcol_core, :]
    remote(part, part, pcol_sem.at[2], pcol_sem.at[6], twin).start()

    rows_in(prowg, prow_sem)

    def pscale(k, _):
        v_ref[k] = -jnp.dot(pinv_ref[...], prowg[k], preferred_element_type=F32).astype(BF)
        return 0

    lax.fori_loop(0, G, pscale, 0)

    rows_left(rowg, row_sem)
    rows_left(prowg, prow_sem)
    quarter = colg.at[:, pl.ds(0, 96), :]
    remote(quarter, quarter, col_sem.at[0], col_sem.at[2], twin).wait_send()
    remote(half_part, half_part, col_sem.at[1], col_sem.at[3], twin).wait_send()
    remote(four, four, pcol_sem.at[0], pcol_sem.at[3], twin).wait_send()
    remote(three, three, pcol_sem.at[1], pcol_sem.at[3], twin).wait_send()
    part = pcol_hbm.at[:, pcol_core, :]
    remote(part, part, pcol_sem.at[2], pcol_sem.at[6], twin).wait_send()
    remote(part, part, pcol_sem.at[2], pcol_sem.at[6], twin).wait_recv()

    for (rh, rc), passing in RELAYS.items():

        @pl.when((h == rh) & (c == rc))
        def _(rh=rh, passing=passing):
            for slot, (hs, _tc) in enumerate(passing):
                part = lbuf.at[pl.ds(0, G - 1 if hs == rh else G)]
                remote(part, part, fsem.at[slot], lsem.at[0], other).wait_send()

    part = sbuf.at[pl.ds(0, G - 1)]
    remote(part, part, ssem.at[0], rsem.at[0], other).wait_send()

    @pl.when(h == 1)
    def _():
        one = sbuf.at[pl.ds(0, 1)]
        remote(one, one, ssem.at[G], rsem.at[0], other).wait_send()

    for d in range(1, G):
        part = sbuf.at[pl.ds(0, G)]
        remote(part, part, ssem.at[d], rsem.at[0], other).wait_send()

    for hs in range(2):
        for cs in range(G):
            dst = recv_hbm.at[hs, :, cs]
            remote(sbuf.at[pl.ds(0, G)], dst, ssem.at[0], rsem.at[hs * G + cs], other).wait_recv()


def exchange(child_map, block, crow, ccol, prow, pcol, cinv, pinv):
    any_space = pl.BlockSpec(memory_space=pl.ANY)
    vmem = pl.BlockSpec(memory_space=pltpu.VMEM)
    smem = pl.BlockSpec(memory_space=pltpu.SMEM)
    dma = pltpu.SemaphoreType.DMA
    return pl.pallas_call(
        exchange_kernel,
        out_shape=(
            pltpu.VMEM((2, G, G, T, T), BF),
            pltpu.VMEM((G, T, T), BF),
            pltpu.VMEM((2 * G, T, T), BF),
        ),
        in_specs=[smem, any_space] + [vmem] * 6,
        out_specs=(any_space, vmem, any_space),
        scratch_shapes=[
            pltpu.VMEM((2, T, G, T), BF),
            pltpu.VMEM((2, T * G, L), F32),
            pltpu.VMEM((G * G, T, T), BF),
            pltpu.VMEM((G, T, T), BF),
            pltpu.VMEM((G, T, T), BF),
            pltpu.VMEM((G, T, T), BF),
            pltpu.VMEM((G, T, T), BF),
            pltpu.VMEM((G * G, T, T), BF),
            pltpu.VMEM((RELAY_SLOTS * G, T, T), BF),
            pltpu.VMEM((G, T, T), BF),
            pltpu.VMEM((G, T, T), BF),
            pltpu.VMEM((G, 32, T), BF),
            pltpu.VMEM((G, 32, T), BF),
            pltpu.VMEM((G, 32, T), BF),
            pltpu.VMEM((2 * G, 16, T), BF),
            pltpu.VMEM((T, T), BF),
            pltpu.VMEM((T, T), BF),
            pltpu.VMEM((G, 32, T), BF),
            pltpu.SMEM((G,), jnp.int32),
            dma((2,)),
            dma((5,)),
            dma((4,)),
            dma((5,)),
            dma((7,)),
            dma((G + 1,)),
            dma((2 * G,)),
            dma((RELAY_SLOTS * G,)),
            dma((RELAY_SLOTS,)),
        ],
        compiler_params=pltpu.CompilerParams(
            collective_id=0, has_side_effects=True, vmem_limit_bytes=37 << 20
        ),
        name="exchange",
    )(child_map, block, crow, ccol, prow, pcol, cinv, pinv)


OUT_SLOTS = 4


def assemble_kernel(
    map_ref, recv_ref, v_ref, pcol_ref, diag_hbm, out_hbm, tile, done, diag_ref, sem, diag_sem
):
    h = lax.axis_index("half")
    r = lax.axis_index("row")
    c = lax.axis_index("col")
    a = pl.program_id(0)
    k = a // 2
    odd = a % 2
    slot = a % OUT_SLOTS
    fetch = pltpu.make_async_copy(diag_hbm, diag_ref, diag_sem)
    pl.when((r == c) & (a == 0))(fetch.start)
    moved = [map_ref[hs, G * k] - 2 * G * k for hs in range(2)]
    live = [(moved[hs] > r).astype(jnp.int32) == odd for hs in range(2)]

    def came(hs, b):
        col = (c - (map_ref[hs, G * b] - 2 * G * b) + G) % G
        return recv_ref[hs, (r - moved[hs] + G) % G, col].astype(F32)

    def put(s, row):
        return pltpu.make_async_copy(done.at[s], out_hbm.at[row], sem.at[s])

    def fill(parts):
        pc = pcol_ref[a].T
        for b in range(G):
            acc = jnp.dot(pc, v_ref[b], preferred_element_type=F32)
            for hs in parts:
                acc = acc + came(hs, b)
            for lane in range(2):
                tile[lane, pl.ds(b, T, stride=G), :] = acc[:, lane * L : lane * L + L]

    pl.when(live[0] & live[1])(lambda: fill((0, 1)))
    pl.when(live[0] & jnp.logical_not(live[1]))(lambda: fill((0,)))
    pl.when(live[1] & jnp.logical_not(live[0]))(lambda: fill((1,)))
    pl.when(jnp.logical_not(live[0] | live[1]))(lambda: fill(()))

    @pl.when((r == c) & (h == odd))
    def _():
        pl.when(k == 0)(fetch.wait)
        i = lax.broadcasted_iota(jnp.int32, (T, T), 0)
        j = lax.broadcasted_iota(jnp.int32, (T, T), 1)
        extra = jnp.where(i == j, diag_ref[a], 0.0)
        for lane in range(2):
            tile[lane, pl.ds(k, T, stride=G), :] += extra[:, lane * L : lane * L + L]

    @pl.when(a >= OUT_SLOTS)
    def _():
        put(slot, a).wait()

    for m in range(8):
        for lane in range(2):
            done[slot, pl.ds(m * 32, 32), :, pl.ds(lane * L, L)] = (
                tile[lane, pl.ds(m * 256, 256), :].reshape(32, G, L).astype(BF)
            )
    put(slot, a).start()

    @pl.when(a == 2 * G - 1)
    def _():
        for s in range(OUT_SLOTS):
            put(s, a).wait()


def assemble(child_map, recv, v, pcol, diag):
    recv, v, pcol = (pltpu.with_memory_space_constraint(x, pltpu.VMEM) for x in (recv, v, pcol))
    child_map, diag = (
        pltpu.with_memory_space_constraint(x, pltpu.HBM) for x in (child_map, diag)
    )
    vmem = pl.BlockSpec(memory_space=pltpu.VMEM)
    return pl.pallas_call(
        assemble_kernel,
        out_shape=jax.ShapeDtypeStruct((2 * G, T, G, T), BF),
        grid_spec=pltpu.PrefetchScalarGridSpec(
            num_scalar_prefetch=1,
            grid=(2 * G,),
            in_specs=[vmem] * 3 + [pl.BlockSpec(memory_space=pl.ANY)],
            out_specs=pl.BlockSpec(memory_space=pl.ANY),
            scratch_shapes=[
                pltpu.VMEM((2, T * G, L), F32),
                pltpu.VMEM((OUT_SLOTS, T, G, T), BF),
                pltpu.VMEM((2 * G, 1, T), F32),
                pltpu.SemaphoreType.DMA((OUT_SLOTS,)),
                pltpu.SemaphoreType.DMA,
            ],
        ),
        compiler_params=pltpu.CompilerParams(vmem_limit_bytes=12 << 20),
        name="assemble",
    )(child_map, recv, v, pcol, diag)


def shards(
    child_block,
    child_row,
    child_col,
    child_pivot_inv,
    child_map,
    parent_row,
    parent_col,
    parent_pivot_inv,
    parent_diag,
):
    recv, v, pcols = exchange(
        child_map,
        child_block.reshape(G, T, G, T),
        child_row.reshape(-1, G, T),
        child_col.reshape(-1, G, T),
        parent_row.reshape(-1, G, T),
        parent_col.reshape(-1, 2 * G, T),
        child_pivot_inv[0],
        parent_pivot_inv,
    )
    out = assemble(child_map, recv, v, pcols, parent_diag)
    return out.reshape(2 * G, 1, T, G, 1, T)


def solution(mesh):
    return jax.shard_map(
        shards,
        mesh=mesh,
        in_specs=(
            P("half", None, "row", None, None, "col", None),
            P("half", "row", None, "col", None),
            P("half", "col", None, "row", None),
            P("half", None, None),
            P(),
            P("row", None, ("half", "col"), None),
            P(("half", "col"), None, "row", None),
            P(),
            P(None, "row", None),
        ),
        out_specs=P(None, "row", None, None, ("half", "col"), None),
        check_vma=False,
    )
```
